32 devices in a mesh: groups: 2 (over x), vel: 16 (over z, y, core).
Axes of the slice: x: 2, y: 2, z: 4, core: 2. Of those that a mesh axis runs over, the one named last changes fastest.
Arguments:
- epoch_maps: bfloat16 [128, 192, 512], P('vel', 'groups'), parts along dimension 1, may hold values from -6 to 6, as said below
- velocity: int32 [16, 2], P('vel'), may hold values from -16 to 16, as said below
- slot_epoch: int32 [64], replicated, may hold values from 0 to 63, each once
- epoch_time: int32 [64], replicated, may hold values from 0 to 127, as said below
Outputs:
- likelihood: float32 [16, 192, 512], P('vel', 'groups'), parts along dimension 1
- best_value: float32 [192, 512], P('groups'), parts along dimension 0
The draws below stay inside these ranges and needn't reach their ends.
There are 2 independent parts, one for each index of `groups`. The reference program is written for one: setup_inputs(seed, part) draws one part's arguments, and reference() takes and returns one part's arrays. A program takes and returns all parts, laid end to end along the dimension named above; an argument that names none is the same for every part. Nothing has to cross between parts.
Inputs may be any that keep to these rules, and one draw needn't show every extreme that they name: `epoch_maps`: the first 64 images are likelihoods, the others weights of at least 0.25 and at most 4. `velocity`: all rows are distinct; rows (16, 16) and (-16, -16) both occur. `epoch_time`: strictly increasing, the first 0 and the last 127. `slot_epoch`: each epoch stands in exactly one slot.
All inputs are finite; a program needn't handle non-finite values.
Results may differ from the reference program's by a relative error of at most 0.0029.
Values may be sent and summed in bfloat16 or wider, within the bound.
A program may use at most 64 MiB of HBM per device.

```python
import jax
import jax.numpy as jnp
from jax import lax

ROWS = 96
COLS = 512
EPOCHS = 64
VMAX = 16
TMAX = 127
VELS = 16


def draw_epoch_maps(key, part):
    first_key, second_key = jax.random.split(jax.random.fold_in(key, 37), 2)
    map_shape = (EPOCHS, ROWS, COLS)
    likelihoods = jnp.clip(jax.random.normal(first_key, map_shape, jnp.float32), -6.0, 6.0)
    weights = jnp.exp(jax.random.uniform(second_key, map_shape, jnp.float32, jnp.log(0.25), jnp.log(4.0)))
    return jnp.concatenate([likelihoods, weights], axis=0).astype(jnp.bfloat16)


def draw_velocity(key, part):
    first_key, second_key = jax.random.split(jax.random.fold_in(key, 11))
    grid_side = 2 * VMAX + 1
    points = grid_side * grid_side
    shuffled = jax.random.permutation(first_key, points).astype(jnp.int32)
    extreme = (shuffled == 0) | (shuffled == points - 1)
    priority = jnp.where(extreme, (shuffled == points - 1).astype(jnp.int32) - 2, jnp.arange(points, dtype=jnp.int32))
    ranked = shuffled[jnp.argsort(priority)]
    chosen = ranked[:VELS]
    chosen = chosen[jax.random.permutation(second_key, VELS)]
    row_rate = chosen // grid_side - VMAX
    column_rate = chosen % grid_side - VMAX
    return jnp.stack([row_rate, column_rate], axis=1).astype(jnp.int32)


def draw_epoch_time(key, part):
    shuffled = jax.random.permutation(jax.random.fold_in(key, 23), TMAX + 1).astype(jnp.int32)
    extreme = (shuffled == 0) | (shuffled == TMAX)
    priority = jnp.where(extreme, (shuffled == TMAX).astype(jnp.int32) - 2, jnp.arange(TMAX + 1, dtype=jnp.int32))
    ranked = shuffled[jnp.argsort(priority)]
    return jnp.sort(ranked[:EPOCHS]).astype(jnp.int32)


def setup_inputs(seed: int = 0, part: int = 0) -> dict:
    splits = jax.random.split(jax.random.key(seed), 5)
    own_keys = jax.random.split(jax.random.fold_in(splits[4], part), 5)
    return {
        "epoch_maps": draw_epoch_maps(jax.random.fold_in(jax.random.fold_in(splits[4], part), 71), part),
        "velocity": draw_velocity(jax.random.fold_in(splits[4], 71), part),
        "slot_epoch": jax.random.permutation(splits[2], EPOCHS).astype(jnp.int32),
        "epoch_time": draw_epoch_time(jax.random.fold_in(splits[4], 71), part),
    }


SPLINE = [[64.0, 256.0, 64.0, 0.0], [27.0, 235.0, 121.0, 1.0], [8.0, 184.0, 184.0, 8.0], [1.0, 121.0, 235.0, 27.0]]
spline_norm = 147456.0
rate_divisor = 32

def spline_taps(offset):
    whole_shift = offset // 4
    fraction = offset - 4 * whole_shift
    spline_table = jnp.array(SPLINE, dtype=jnp.float32)
    return (whole_shift.astype(jnp.int32), spline_table[fraction])

def shift_axis(epoch_image, whole_shift, weights, margin, axis_number):
    widths = [(0, 0), (0, 0), (0, 0)]
    widths[axis_number] = (margin, margin)
    padded = jnp.pad(epoch_image, widths)
    length = epoch_image.shape[axis_number]
    result = jnp.zeros(epoch_image.shape, jnp.float32)
    for tap_number in range(4):
        position = (margin - 1 + tap_number + whole_shift).astype(jnp.int32)
        result = result + weights[tap_number] * lax.dynamic_slice_in_dim(padded, position, length, axis_number)
    return result

def one_epoch(epoch_image, row_offset, column_offset, margin):
    row_whole, row_weights = spline_taps(row_offset)
    rows_done = shift_axis(epoch_image.astype(jnp.float32), row_whole, row_weights, margin, 1)
    rounded = lax.optimization_barrier(rows_done.astype(jnp.bfloat16))
    column_whole, column_weights = spline_taps(column_offset)
    return shift_axis(rounded.astype(jnp.float32), column_whole, column_weights, margin, 2)

def reference(epoch_maps, velocity, slot_epoch, epoch_time):
    margin = VMAX * TMAX // 128 + 3
    images = jnp.stack([epoch_maps[:EPOCHS], epoch_maps[EPOCHS:]], axis=1)
    slot_time = epoch_time[slot_epoch]

    def per_velocity(rate_pair):
        row_offsets = rate_pair[0] * slot_time // rate_divisor
        column_offsets = rate_pair[1] * slot_time // rate_divisor
        stacks = jax.vmap(one_epoch, in_axes=(0, 0, 0, None))(images, row_offsets, column_offsets, margin)
        stack_sums = lax.optimization_barrier(jnp.sum(stacks, axis=0)) / spline_norm
        return stack_sums[0] / jnp.sqrt(stack_sums[1] + 1.0)
    likelihood = lax.map(per_velocity, velocity)
    return (likelihood, lax.optimization_barrier(jnp.max(likelihood, axis=0)))
```

```python
import functools
import math

import jax
import jax.numpy as jnp
from jax import lax
from jax.experimental import pallas as pl
from jax.experimental.pallas import tpu as pltpu
from jax.sharding import PartitionSpec as P

SPLINE = (
    (64.0, 256.0, 64.0, 0.0),
    (27.0, 235.0, 121.0, 1.0),
    (8.0, 184.0, 184.0, 8.0),
    (1.0, 121.0, 235.0, 27.0),
)
spline_norm = 147456.0
rate_divisor = 32
HALO = 64
LANES = 128
REACH = 16
EDGE = 8
FORWARD_LAG = 3
LIKE_LAG = 6


def scalar_taps(offset):
    whole = offset >> 2
    fraction = offset & 3
    taps = []
    for tap in range(4):
        value = jnp.float32(SPLINE[3][tap])
        for level in range(3):
            value = jnp.where(fraction == level, jnp.float32(SPLINE[level][tap]), value)
        taps.append(value)
    return whole, taps


def band(distance, offset):
    whole, taps = scalar_taps(offset)
    relative = distance - whole
    out = jnp.where(relative == 3, taps[3], 0.0)
    for tap in (2, 1, 0):
        out = jnp.where(relative == tap, taps[tap], out)
    return out.astype(jnp.bfloat16)


def stack_one(rate_row, rate_col, times, padded, bands, rows_done, count, rows, cols):
    blocks = cols // LANES
    row_distance = (
        lax.broadcasted_iota(jnp.int32, (rows, rows), 1)
        - lax.broadcasted_iota(jnp.int32, (rows, rows), 0)
        + 1
    )
    col_distance = (
        lax.broadcasted_iota(jnp.int32, (2 * LANES, LANES), 0)
        - lax.broadcasted_iota(jnp.int32, (2 * LANES, LANES), 1)
        + (1 - HALO)
    )
    for s in range(count):
        row_band = band(row_distance, (rate_row * times(s)) >> 5)
        bands[pl.ds(s * 2 * LANES, 2 * LANES), :] = band(
            col_distance, (rate_col * times(s)) >> 5
        )
        rows_done[s] = jnp.dot(
            row_band, padded[s], preferred_element_type=jnp.float32
        ).astype(jnp.bfloat16)
    lhs = jnp.concatenate(
        [
            jnp.concatenate(
                [rows_done[s, :, b * LANES : (b + 2) * LANES] for s in range(count)], axis=1
            )
            for b in range(blocks)
        ],
        axis=0,
    )
    return jnp.dot(lhs, bands[...], preferred_element_type=jnp.float32)


def pad_images(images, padded, start, count):
    zeros = jnp.zeros((images.shape[1], HALO), jnp.bfloat16)
    for s in range(count):
        padded[start + s] = jnp.concatenate([zeros, images[s], zeros], axis=1)


def stack_kernel(count, rows, cols, vel_ref, time_ref, images, out, padded, bands, rows_done):
    pad_images(images, padded, 0, count)
    hypotheses = out.shape[0]

    @pl.loop(0, hypotheses)
    def _(v):
        total = stack_one(
            vel_ref[v, 0],
            vel_ref[v, 1],
            lambda s: time_ref[s],
            padded,
            bands,
            rows_done,
            count,
            rows,
            cols,
        )
        for b in range(cols // LANES):
            out[v, :, b * LANES : (b + 1) * LANES] = total[b * rows : (b + 1) * rows].astype(
                out.dtype
            )


def tap_select(relative, taps):
    out = jnp.zeros(relative.shape, jnp.float32)
    for tap in range(4):
        if taps[tap]:
            out = jnp.where(relative == tap, jnp.float32(taps[tap]), out)
    return out


def fused_kernel(
    chips,
    epochs,
    count,
    rows,
    cols,
    se_ref,
    et_ref,
    vel_ref,
    images,
    out_ref,
    peer_images,
    row_taps,
    table,
    base,
    lhs,
    bands,
    vel_all,
    part_send,
    part_recv,
    far_own,
    hop_recv,
    far_send,
    like_send,
    max_send,
    max_recv,
    best_send,
    image_sems,
    vel_send,
    vel_recv,
    part_ssem,
    part_rsem,
    hop_ssem,
    hop_rsem,
    max_sems,
    like_ssem,
    like_rsem,
    best_ssem,
    best_rsem,
):
    like_out, best_out = out_ref.at[pl.ds(0, 1)], out_ref.at[1]
    me = lax.axis_index("vel")
    chip, core = me // 2, me % 2
    sibling = chip * 2 + 1 - core
    blocks = cols // LANES
    levels, near_levels = chips // 2, chips // 4
    half = chips // 2
    slice_rows = rows * blocks // chips
    level, column = chip // 2, chip % 2
    mate = level * 2 + 1 - column
    near0 = level // near_levels * half
    far_level = near_levels - level // near_levels * near_levels
    images_all = 2 * count

    def window(owner):
        return (
            pl.ds(pl.multiple_of(owner // blocks * slice_rows, slice_rows), slice_rows),
            pl.ds(pl.multiple_of(owner % blocks * LANES, LANES), LANES),
        )

    def slot(owner):
        return owner % 2 * levels + owner // 2

    def remote(source, target, send, receive, device):
        return pltpu.make_async_remote_copy(
            src_ref=source,
            dst_ref=target,
            send_sem=send,
            recv_sem=receive,
            device_id={"vel": device},
            device_id_type=pl.DeviceIdType.MESH,
        )

    def rail(other):
        return other * 2 + core

    def each_rail(body):
        @pl.loop(1, chips)
        def _(step):
            body(lax.rem(chip + step, chips))

    def each_near(body):
        @pl.loop(1, half)
        def _(step):
            body(near0 + lax.rem(chip - near0 + step, half))

    def greet(device):
        pl.semaphore_signal(
            barrier, inc=1, device_id={"vel": device}, device_id_type=pl.DeviceIdType.MESH
        )

    barrier = pltpu.get_barrier_semaphore()
    greet(sibling)
    each_rail(lambda other: greet(rail(other)))

    span = rows + 2 * EDGE
    relative = (
        lax.broadcasted_iota(jnp.int32, (span, rows), 1)
        - lax.broadcasted_iota(jnp.int32, (span, rows), 0)
        + (EDGE + 1)
    )
    for f in range(4):
        row_taps[f * span : (f + 1) * span, :] = tap_select(relative, SPLINE[f]).astype(jnp.bfloat16)
    base_shape = base.shape[2:]
    for h in range(2):
        distance = (
            lax.broadcasted_iota(jnp.int32, base_shape, 0)
            - lax.broadcasted_iota(jnp.int32, base_shape, 1)
            + (HALO + 1 - REACH - h * LANES)
        )
        for f in range(4):
            base[f, h] = tap_select(distance, SPLINE[f])
    blank = jnp.zeros((blocks, REACH - EDGE, LANES), jnp.float32)

    def filter_rows(source, s, index):
        mixed = jnp.dot(row_taps[...], source[s], preferred_element_type=jnp.float32)
        mixed = mixed.astype(jnp.bfloat16).astype(jnp.float32)
        for f in range(4):
            table[index * 4 + f, :, 0 : REACH - EDGE] = blank
            table[index * 4 + f, :, REACH + rows + EDGE : rows + 2 * REACH] = blank
            for b in range(blocks):
                table[index * 4 + f, b, REACH - EDGE : REACH + rows + EDGE] = mixed[
                    f * span : (f + 1) * span, b * LANES : (b + 1) * LANES
                ]

    early = count // 2

    @pl.loop(0, early)
    def _(s):
        filter_rows(images, s, s)

    max_send[...] = jnp.full_like(max_send, -jnp.inf)
    pl.semaphore_wait(barrier, chips)

    def vel_copy(source, target, other):
        return remote(vel_ref, vel_all.at[target], vel_send.at[source], vel_recv.at[target], rail(other))

    swap = remote(images, peer_images, image_sems.at[0], image_sems.at[1], sibling)
    swap.start()
    each_rail(lambda other: vel_copy(other, chip, other).start())
    vel_all[chip, 0, 0] = vel_ref[0, 0]
    vel_all[chip, 0, 1] = vel_ref[0, 1]

    @pl.loop(early, count)
    def _(s):
        filter_rows(images, s, s)

    swap.wait_recv()

    @pl.loop(0, count)
    def _(s):
        filter_rows(peer_images, s, s + count)

    first = lax.rem(me * count, epochs)
    peer_first = lax.rem(sibling * count, epochs)

    def time(s):
        at = first + s if s < count else peer_first + (s - count)
        return et_ref[se_ref[at]]

    def stack(rate_row, rate_col):
        for s in range(images_all):
            qr = (rate_row * time(s)) >> 5
            qc = (rate_col * time(s)) >> 5
            for b in range(blocks):
                lhs[b * rows : (b + 1) * rows, s * LANES : (s + 1) * LANES] = table[
                    s * 4 + (qr & 3), b, pl.ds((qr >> 2) + REACH, rows), :
                ].astype(jnp.bfloat16)
            for h in range(2):
                bands[s * LANES : (s + 1) * LANES, h * LANES : (h + 1) * LANES] = base[
                    qc & 3, h, pl.ds(REACH - (qc >> 2), LANES), :
                ].astype(jnp.bfloat16)
        wide = jnp.dot(lhs[...], bands[...], preferred_element_type=jnp.float32)
        tiles = []
        for t in range(blocks + 1):
            tile = None
            if t < blocks:
                tile = wide[t * rows : (t + 1) * rows, :LANES]
            if t:
                right = wide[(t - 1) * rows : t * rows, LANES:]
                tile = right if tile is None else tile + right
            tiles.append(pltpu.roll(tile, HALO, 1))
        left = lax.broadcasted_iota(jnp.int32, (rows, LANES), 1) < HALO
        return [jnp.where(left, tiles[b], tiles[b + 1]) for b in range(blocks)]

    def part_copy(v, source, other):
        return remote(
            part_send.at[v, slot(other)],
            part_recv.at[v, source],
            part_ssem.at[v, other],
            part_rsem.at[v, source],
            rail(other),
        )

    def far_copy(v, step, source):
        other = (far_level + step) * 2 + column
        return remote(
            far_send.at[v, step],
            part_recv.at[v, source],
            part_ssem.at[v, other],
            part_rsem.at[v, source],
            rail(other),
        )

    def hop_copy(v):
        return remote(
            part_send.at[v, pl.ds((1 - column) * levels + far_level, near_levels)],
            hop_recv.at[v],
            hop_ssem.at[v],
            hop_rsem.at[v],
            rail(mate),
        )

    def like_copy(v, owner):
        return remote(
            like_send.at[v],
            like_out.at[0, window(owner)[0], window(owner)[1]],
            like_ssem.at[v],
            like_rsem.at[owner],
            rail(v),
        )

    def forward(v):
        hop_copy(v).wait_recv()

        @pl.loop(0, near_levels)
        def _(step):
            total = far_own[v, column * levels + far_level + step] + hop_recv[v, step].astype(jnp.float32)
            far_send[v, step] = total.astype(jnp.bfloat16)
            far_copy(v, step, chip).start()

    def finish_like(v):
        each_near(lambda other: part_copy(v, other, other).wait_recv())

        @pl.loop(0, near_levels)
        def _(step):
            far_copy(v, 0, (far_level + step) * 2 + column).wait_recv()

        near = far_own[v, slot(chip)]
        for step in range(1, half):
            near = near + part_recv[v, near0 + lax.rem(chip - near0 + step, half)].astype(jnp.float32)
        far = part_recv[v, far_level * 2 + column].astype(jnp.float32)
        for step in range(1, near_levels):
            far = far + part_recv[v, (far_level + step) * 2 + column].astype(jnp.float32)
        first_kind = near0 == 0
        signal = jnp.where(first_kind, near, far) / spline_norm
        weight = jnp.where(first_kind, far, near) / spline_norm
        value = signal / jnp.sqrt(weight + 1.0)
        max_send[...] = jnp.maximum(max_send[...], value)
        like_send[v] = value

        @pl.when(v != chip)
        def _():
            like_copy(v, chip).start()

    @pl.loop(0, chips)
    def _(i):
        begun = (i + chips - 1) // chips
        v = (i - 1 + (i - 1 - chip + chips) // chips) * begun + chip * (1 - begun)

        @pl.when(i >= 1)
        def _():
            vel_copy(v, v, v).wait_recv()

        total = stack(vel_all[v, 0, 0], vel_all[v, 0, 1])
        for owner in range(chips):
            start = owner // blocks * slice_rows
            piece = total[owner % blocks][start : start + slice_rows]
            at = owner % 2 * levels + owner // 2
            far_own[v, at] = piece
            part_send[v, at] = piece.astype(jnp.bfloat16)

        hop_copy(v).start()
        each_near(lambda other: part_copy(v, chip, other).start())

        @pl.when(i >= FORWARD_LAG)
        def _():
            forward(i - FORWARD_LAG)

        @pl.when(i >= LIKE_LAG)
        def _():
            finish_like(i - LIKE_LAG)

    gap = LIKE_LAG - FORWARD_LAG

    @pl.loop(chips, chips + FORWARD_LAG)
    def _(i):
        forward(i - FORWARD_LAG)

        @pl.when(i >= LIKE_LAG)
        def _():
            finish_like(i - LIKE_LAG)

    @pl.loop(chips - gap, chips)
    def _(v):
        finish_like(v)

    meet = remote(max_send, max_recv, max_sems.at[0], max_sems.at[1], sibling)
    meet.start()
    like_out[0, window(chip)[0], window(chip)[1]] = like_send[chip]
    meet.wait()
    best_send[...] = jnp.maximum(max_send[...], max_recv[...])

    def best_copy(owner, other):
        return remote(
            best_send,
            best_out.at[window(owner)[0], window(owner)[1]],
            best_ssem.at[other],
            best_rsem.at[owner],
            rail(other),
        )

    each_rail(lambda other: best_copy(chip, other).start())
    best_out[window(chip)[0], window(chip)[1]] = best_send[...]

    @pl.loop(0, chips)
    def _(v):
        each_near(lambda other: part_copy(v, chip, other).wait_send())
        hop_copy(v).wait_send()

        @pl.loop(0, near_levels)
        def _(step):
            far_copy(v, step, chip).wait_send()

    swap.wait_send()

    def finish(other):
        vel_copy(other, chip, other).wait_send()
        like_copy(other, other).wait()
        best_copy(other, other).wait()

    each_rail(finish)


def fused(n, epoch_maps, velocity, slot_epoch, epoch_time):
    count, rows, cols = epoch_maps.shape
    epochs = slot_epoch.shape[0]
    chips = n // 2
    half, quarter = chips // 2, chips // 4
    blocks = cols // LANES
    slice_rows = rows * blocks // chips
    smem = pl.BlockSpec(memory_space=pltpu.SMEM)
    vmem = pl.BlockSpec(memory_space=pltpu.VMEM)
    f32, bf16 = jnp.float32, jnp.bfloat16
    dma = pltpu.SemaphoreType.DMA
    both = pl.pallas_call(
        functools.partial(fused_kernel, chips, epochs, count, rows, cols),
        out_shape=jax.ShapeDtypeStruct((2, rows, cols), f32),
        in_specs=[smem, smem, smem, vmem],
        out_specs=vmem,
        scratch_shapes=[
            pltpu.VMEM((count, rows, cols), bf16),
            pltpu.VMEM((4 * (rows + 2 * EDGE), rows), bf16),
            pltpu.VMEM((2 * count * 4, blocks, rows + 2 * REACH, LANES), f32),
            pltpu.VMEM((4, 2, LANES + 2 * REACH, LANES), f32),
            pltpu.VMEM((blocks * rows, 2 * count * LANES), bf16),
            pltpu.VMEM((2 * count * LANES, 2 * LANES), bf16),
            pltpu.SMEM((chips, 1, 2), jnp.int32),
            pltpu.VMEM((chips, chips, slice_rows, LANES), bf16),
            pltpu.VMEM((chips, chips, slice_rows, LANES), bf16),
            pltpu.VMEM((chips, chips, slice_rows, LANES), f32),
            pltpu.VMEM((chips, quarter, slice_rows, LANES), bf16),
            pltpu.VMEM((chips, quarter, slice_rows, LANES), bf16),
            pltpu.VMEM((chips, slice_rows, LANES), f32),
            pltpu.VMEM((slice_rows, LANES), f32),
            pltpu.VMEM((slice_rows, LANES), f32),
            pltpu.VMEM((slice_rows, LANES), f32),
            dma((2,)),
            dma((chips,)),
            dma((chips,)),
            dma((chips, chips)),
            dma((chips, chips)),
            dma((chips,)),
            dma((chips,)),
            dma((2,)),
            dma((chips,)),
            dma((chips,)),
            dma((chips,)),
            dma((chips,)),
        ],
        compiler_params=pltpu.CompilerParams(collective_id=0, has_side_effects=True),
    )(slot_epoch, epoch_time, velocity, epoch_maps)
    return (both[:1], both[1])


def fits(n, epoch_maps, velocity, epochs):
    count, rows, cols = epoch_maps.shape
    chips = n // 2
    blocks = cols // LANES
    return (
        n % 4 == 0
        and velocity.shape[0] == 1
        and n * count == 2 * epochs
        and cols % LANES == 0
        and chips % blocks == 0
        and rows % (chips // blocks * 16) == 0
    )


def local(n, epoch_maps, velocity, slot_epoch, epoch_time):
    count, rows, cols = epoch_maps.shape
    epochs = slot_epoch.shape[0]
    if fits(n, epoch_maps, velocity, epochs):
        return fused(n, epoch_maps, velocity, slot_epoch, epoch_time)
    me = lax.axis_index("vel")
    vels = lax.all_gather(velocity, "vel", axis=0, tiled=True)
    first = lax.rem(me * count, epochs)
    slots = lax.dynamic_slice_in_dim(slot_epoch, first, count, 0)
    times = epoch_time[slots]
    partial = pl.pallas_call(
        functools.partial(stack_kernel, count, rows, cols),
        out_shape=jax.ShapeDtypeStruct((vels.shape[0], rows, cols), jnp.bfloat16),
        in_specs=[
            pl.BlockSpec(memory_space=pltpu.SMEM),
            pl.BlockSpec(memory_space=pltpu.SMEM),
            pl.BlockSpec(memory_space=pltpu.VMEM),
        ],
        out_specs=pl.BlockSpec(memory_space=pltpu.VMEM),
        scratch_shapes=[
            pltpu.VMEM((count, rows, cols + 2 * HALO), jnp.bfloat16),
            pltpu.VMEM((count * 2 * LANES, LANES), jnp.bfloat16),
            pltpu.VMEM((count, rows, cols + 2 * HALO), jnp.bfloat16),
        ],
    )(vels, times, epoch_maps)
    mine = velocity.shape[0]
    received = lax.all_to_all(partial, "vel", 0, 0, tiled=True)
    received = received.reshape(2, n // 2, mine, rows, cols)
    stack_sums = jnp.sum(received.astype(jnp.float32), axis=1) / spline_norm
    likelihood = stack_sums[0] / jnp.sqrt(stack_sums[1] + 1.0)
    best_value = lax.pmax(jnp.max(likelihood, axis=0), "vel")
    return (likelihood, best_value)


def solution(mesh):
    return jax.shard_map(
        functools.partial(local, mesh.shape["vel"]),
        mesh=mesh,
        in_specs=(P("vel", "groups", None), P("vel", None), P(), P()),
        out_specs=(P("vel", "groups", None), P("groups", None)),
        check_vma=False,
    )
```

```python
import functools
import math

import jax
import jax.numpy as jnp
from jax import lax
from jax.experimental import pallas as pl
from jax.experimental.pallas import tpu as pltpu
from jax.sharding import PartitionSpec as P

SPLINE = (
    (64.0, 256.0, 64.0, 0.0),
    (27.0, 235.0, 121.0, 1.0),
    (8.0, 184.0, 184.0, 8.0),
    (1.0, 121.0, 235.0, 27.0),
)
spline_norm = 147456.0
rate_divisor = 32
HALO = 64
LANES = 128
REACH = 16
EDGE = 8
FIT_PIXELS = 1 << 19
FORWARD_LAG = 4


def scalar_taps(offset):
    whole = offset >> 2
    fraction = offset & 3
    taps = []
    for tap in range(4):
        value = jnp.float32(SPLINE[3][tap])
        for level in range(3):
            value = jnp.where(fraction == level, jnp.float32(SPLINE[level][tap]), value)
        taps.append(value)
    return whole, taps


def band(distance, offset):
    whole, taps = scalar_taps(offset)
    relative = distance - whole
    out = jnp.where(relative == 3, taps[3], 0.0)
    for tap in (2, 1, 0):
        out = jnp.where(relative == tap, taps[tap], out)
    return out.astype(jnp.bfloat16)


def stack_one(rate_row, rate_col, times, padded, bands, rows_done, count, rows, cols):
    blocks = cols // LANES
    row_distance = (
        lax.broadcasted_iota(jnp.int32, (rows, rows), 1)
        - lax.broadcasted_iota(jnp.int32, (rows, rows), 0)
        + 1
    )
    col_distance = (
        lax.broadcasted_iota(jnp.int32, (2 * LANES, LANES), 0)
        - lax.broadcasted_iota(jnp.int32, (2 * LANES, LANES), 1)
        + (1 - HALO)
    )
    for s in range(count):
        row_band = band(row_distance, (rate_row * times(s)) >> 5)
        bands[pl.ds(s * 2 * LANES, 2 * LANES), :] = band(
            col_distance, (rate_col * times(s)) >> 5
        )
        rows_done[s] = jnp.dot(
            row_band, padded[s], preferred_element_type=jnp.float32
        ).astype(jnp.bfloat16)
    lhs = jnp.concatenate(
        [
            jnp.concatenate(
                [rows_done[s, :, b * LANES : (b + 2) * LANES] for s in range(count)], axis=1
            )
            for b in range(blocks)
        ],
        axis=0,
    )
    return jnp.dot(lhs, bands[...], preferred_element_type=jnp.float32)


def pad_images(images, padded, start, count):
    zeros = jnp.zeros((images.shape[1], HALO), jnp.bfloat16)
    for s in range(count):
        padded[start + s] = jnp.concatenate([zeros, images[s], zeros], axis=1)


def stack_kernel(count, rows, cols, vel_ref, time_ref, images, out, padded, bands, rows_done):
    pad_images(images, padded, 0, count)
    hypotheses = out.shape[0]

    @pl.loop(0, hypotheses)
    def _(v):
        total = stack_one(
            vel_ref[v, 0],
            vel_ref[v, 1],
            lambda s: time_ref[s],
            padded,
            bands,
            rows_done,
            count,
            rows,
            cols,
        )
        for b in range(cols // LANES):
            out[v, :, b * LANES : (b + 1) * LANES] = total[b * rows : (b + 1) * rows].astype(
                out.dtype
            )


def tap_select(relative, taps):
    out = jnp.zeros(relative.shape, jnp.float32)
    for tap in range(4):
        if taps[tap]:
            out = jnp.where(relative == tap, jnp.float32(taps[tap]), out)
    return out


def fused_kernel(
    chips,
    epochs,
    count,
    rows,
    cols,
    se_ref,
    et_ref,
    vel_ref,
    images,
    out_ref,
    peer_images,
    row_taps,
    table,
    base,
    lhs,
    bands,
    vel_all,
    part_send,
    part_recv,
    own,
    far_send,
    far_recv,
    like_send,
    best_mine,
    max_recv,
    cross_send,
    cross_recv,
    best_send,
    image_sems,
    vel_send,
    vel_recv,
    part_ssem,
    part_rsem,
    far_ssem,
    far_rsem,
    max_sems,
    like_ssem,
    like_rsem,
    best_ssem,
    best_rsem,
):
    like_out, best_out = out_ref.at[pl.ds(0, 1)], out_ref.at[1]
    me = lax.axis_index("vel")
    chip, core = me // 2, me % 2
    sibling = chip * 2 + 1 - core
    blocks = cols // LANES
    near_levels = chips // 4
    half = chips // 2
    slice_rows = rows * blocks // half
    share_rows = slice_rows // 2
    near0 = chip // half * half
    far0 = half - near0
    place = chip - near0
    images_all = 2 * count

    def slot(owner):
        return owner % 2 * near_levels + owner // 2 % near_levels

    def window(owner, begin, size):
        at = slot(owner)
        start = at // blocks * slice_rows + begin
        return (
            pl.ds(pl.multiple_of(start, share_rows), size),
            pl.ds(pl.multiple_of(at % blocks * LANES, LANES), LANES),
        )

    def remote(source, target, send, receive, device):
        return pltpu.make_async_remote_copy(
            src_ref=source,
            dst_ref=target,
            send_sem=send,
            recv_sem=receive,
            device_id={"vel": device},
            device_id_type=pl.DeviceIdType.MESH,
        )

    def rail(other):
        return other * 2 + core

    def each_rail(body):
        @pl.loop(1, chips)
        def _(step):
            body(lax.rem(chip + step, chips))

    def each_near(body):
        @pl.loop(1, half)
        def _(step):
            body(near0 + lax.rem(chip - near0 + step, half))

    def greet(device):
        pl.semaphore_signal(
            barrier, inc=1, device_id={"vel": device}, device_id_type=pl.DeviceIdType.MESH
        )

    barrier = pltpu.get_barrier_semaphore()
    greet(sibling)
    each_rail(lambda other: greet(rail(other)))
    each_near(lambda other: greet(other * 2 + 1 - core))

    span = rows + 2 * EDGE
    relative = (
        lax.broadcasted_iota(jnp.int32, (span, rows), 1)
        - lax.broadcasted_iota(jnp.int32, (span, rows), 0)
        + (EDGE + 1)
    )
    for f in range(4):
        row_taps[f * span : (f + 1) * span, :] = tap_select(relative, SPLINE[f]).astype(jnp.bfloat16)
    base_shape = base.shape[2:]
    for h in range(2):
        distance = (
            lax.broadcasted_iota(jnp.int32, base_shape, 0)
            - lax.broadcasted_iota(jnp.int32, base_shape, 1)
            + (HALO + 1 - REACH - h * LANES)
        )
        for f in range(4):
            base[f, h] = tap_select(distance, SPLINE[f])
    blank = jnp.zeros((blocks, REACH - EDGE, LANES), jnp.float32)

    def filter_rows(source, s, index):
        mixed = jnp.dot(row_taps[...], source[s], preferred_element_type=jnp.float32)
        mixed = mixed.astype(jnp.bfloat16).astype(jnp.float32)
        for f in range(4):
            table[index * 4 + f, :, 0 : REACH - EDGE] = blank
            table[index * 4 + f, :, REACH + rows + EDGE : rows + 2 * REACH] = blank
            for b in range(blocks):
                table[index * 4 + f, b, REACH - EDGE : REACH + rows + EDGE] = mixed[
                    f * span : (f + 1) * span, b * LANES : (b + 1) * LANES
                ]

    early = count // 2

    @pl.loop(0, early)
    def _(s):
        filter_rows(images, s, s)

    best_mine[...] = jnp.full_like(best_mine, -jnp.inf)
    pl.semaphore_wait(barrier, chips + half - 1)

    def vel_copy(source, target, other):
        return remote(vel_ref, vel_all.at[target], vel_send.at[source], vel_recv.at[target], rail(other))

    swap = remote(images, peer_images, image_sems.at[0], image_sems.at[1], sibling)
    swap.start()
    each_rail(lambda other: vel_copy(other, chip, other).start())
    vel_all[chip, 0, 0] = vel_ref[0, 0]
    vel_all[chip, 0, 1] = vel_ref[0, 1]

    @pl.loop(early, count)
    def _(s):
        filter_rows(images, s, s)

    swap.wait_recv()

    @pl.loop(0, count)
    def _(s):
        filter_rows(peer_images, s, s + count)

    first = lax.rem(me * count, epochs)
    peer_first = lax.rem(sibling * count, epochs)

    def time(s):
        at = first + s if s < count else peer_first + (s - count)
        return et_ref[se_ref[at]]

    def stack(rate_row, rate_col):
        for s in range(images_all):
            qr = (rate_row * time(s)) >> 5
            qc = (rate_col * time(s)) >> 5
            for b in range(blocks):
                lhs[b * rows : (b + 1) * rows, s * LANES : (s + 1) * LANES] = table[
                    s * 4 + (qr & 3), b, pl.ds((qr >> 2) + REACH, rows), :
                ].astype(jnp.bfloat16)
            for h in range(2):
                bands[s * LANES : (s + 1) * LANES, h * LANES : (h + 1) * LANES] = base[
                    qc & 3, h, pl.ds(REACH - (qc >> 2), LANES), :
                ].astype(jnp.bfloat16)
        wide = jnp.dot(lhs[...], bands[...], preferred_element_type=jnp.float32)
        tiles = []
        for t in range(blocks + 1):
            tile = None
            if t < blocks:
                tile = wide[t * rows : (t + 1) * rows, :LANES]
            if t:
                right = wide[(t - 1) * rows : t * rows, LANES:]
                tile = right if tile is None else tile + right
            tiles.append(pltpu.roll(tile, HALO, 1))
        left = lax.broadcasted_iota(jnp.int32, (rows, LANES), 1) < HALO
        return [jnp.where(left, tiles[b], tiles[b + 1]) for b in range(blocks)]

    def part_copy(v, source, other):
        return remote(
            part_send.at[v, slot(other)],
            part_recv.at[v, source - near0],
            part_ssem.at[v, other - near0],
            part_rsem.at[v, source - near0],
            rail(other),
        )

    def far_copy(f):
        return remote(
            far_send.at[f], far_recv.at[f], far_ssem.at[f], far_rsem.at[f], rail(far0 + place)
        )

    def like_copy(o, owner):
        where = window(owner, 0, slice_rows)
        return remote(
            like_send.at[o],
            like_out.at[0, where[0], where[1]],
            like_ssem.at[o],
            like_rsem.at[owner],
            rail(near0 + o),
        )

    def near_sum(v):
        each_near(lambda other: part_copy(v, other, other).wait_recv())
        total = own[v, slot(chip)]
        for step in range(1, half):
            total = total + part_recv[v, lax.rem(place + step, half)].astype(jnp.float32)
        return total

    def forward(f):
        far_send[f] = near_sum(far0 + f).astype(jnp.bfloat16)
        far_copy(f).start()

    def finish_like(o):
        near = near_sum(near0 + o)
        far_copy(o).wait_recv()
        far = far_recv[o].astype(jnp.float32)
        first_kind = near0 == 0
        signal = jnp.where(first_kind, near, far) / spline_norm
        weight = jnp.where(first_kind, far, near) / spline_norm
        value = signal / jnp.sqrt(weight + 1.0)
        best_mine[...] = jnp.maximum(best_mine[...], value)
        like_send[o] = value

        @pl.when(o != place)
        def _():
            like_copy(o, chip).start()

    @pl.loop(0, chips)
    def _(i):
        begun = (i + chips - 1) // chips
        later = (i - 1 - half + chips) // chips
        turn = (i - 1 - half) * later
        near_v = near0 + (turn + (turn - place + half) // half) * later + place * (1 - begun)
        is_far = begun - later
        v = is_far * (far0 + i - 1) + (1 - is_far) * near_v

        @pl.when(i >= 1)
        def _():
            vel_copy(v, v, v).wait_recv()

        total = stack(vel_all[v, 0, 0], vel_all[v, 0, 1])
        for at in range(half):
            start = at // blocks * slice_rows
            piece = total[at % blocks][start : start + slice_rows]
            own[v, at] = piece
            part_send[v, at] = piece.astype(jnp.bfloat16)

        each_near(lambda other: part_copy(v, chip, other).start())

        @pl.when(i >= 1 + FORWARD_LAG)
        def _():
            forward(i - 1 - FORWARD_LAG)

    @pl.loop(chips - 1 - FORWARD_LAG, half)
    def _(f):
        forward(f)

    @pl.loop(0, half)
    def _(o):
        finish_like(o)

    other_core = 1 - core
    mine = pl.ds(pl.multiple_of(core * share_rows, share_rows), share_rows)
    theirs = pl.ds(pl.multiple_of(other_core * share_rows, share_rows), share_rows)
    meet = remote(best_mine.at[theirs], max_recv, max_sems.at[0], max_sems.at[1], sibling)
    meet.start()
    where = window(chip, 0, slice_rows)
    like_out[0, where[0], where[1]] = like_send[place]
    meet.wait_recv()
    cross_send[...] = jnp.maximum(best_mine[mine, :], max_recv[...])
    cross = remote(cross_send, cross_recv, max_sems.at[2], max_sems.at[3], rail(far0 + place))
    cross.start()
    cross.wait_recv()
    best_send[...] = jnp.maximum(cross_send[...], cross_recv[...])

    def best_copy(source, target):
        where = window(source // 2, source % 2 * share_rows, share_rows)
        return remote(
            best_send,
            best_out.at[where[0], where[1]],
            best_ssem.at[target],
            best_rsem.at[source],
            near0 * 2 + target,
        )

    seat = place * 2 + core

    def each_seat(body):
        @pl.loop(1, 2 * half)
        def _(step):
            body(lax.rem(seat + step, 2 * half))

    each_seat(lambda target: best_copy(seat, target).start())
    where = window(chip, core * share_rows, share_rows)
    best_out[where[0], where[1]] = best_send[...]

    @pl.loop(0, chips)
    def _(v):
        each_near(lambda other: part_copy(v, chip, other).wait_send())

    @pl.loop(0, half)
    def _(f):
        far_copy(f).wait_send()

    swap.wait_send()
    meet.wait_send()
    cross.wait_send()
    each_rail(lambda other: vel_copy(other, chip, other).wait_send())
    each_near(lambda other: like_copy(other - near0, other).wait())
    each_seat(lambda other: best_copy(other, other).wait())


def fused(n, epoch_maps, velocity, slot_epoch, epoch_time):
    count, rows, cols = epoch_maps.shape
    epochs = slot_epoch.shape[0]
    chips = n // 2
    half = chips // 2
    blocks = cols // LANES
    slice_rows = rows * blocks // half
    smem = pl.BlockSpec(memory_space=pltpu.SMEM)
    vmem = pl.BlockSpec(memory_space=pltpu.VMEM)
    f32, bf16 = jnp.float32, jnp.bfloat16
    dma = pltpu.SemaphoreType.DMA
    both = pl.pallas_call(
        functools.partial(fused_kernel, chips, epochs, count, rows, cols),
        out_shape=jax.ShapeDtypeStruct((2, rows, cols), f32),
        in_specs=[smem, smem, smem, vmem],
        out_specs=vmem,
        scratch_shapes=[
            pltpu.VMEM((count, rows, cols), bf16),
            pltpu.VMEM((4 * (rows + 2 * EDGE), rows), bf16),
            pltpu.VMEM((2 * count * 4, blocks, rows + 2 * REACH, LANES), f32),
            pltpu.VMEM((4, 2, LANES + 2 * REACH, LANES), f32),
            pltpu.VMEM((blocks * rows, 2 * count * LANES), bf16),
            pltpu.VMEM((2 * count * LANES, 2 * LANES), bf16),
            pltpu.SMEM((chips, 1, 2), jnp.int32),
            pltpu.VMEM((chips, half, slice_rows, LANES), bf16),
            pltpu.VMEM((chips, half, slice_rows, LANES), bf16),
            pltpu.VMEM((chips, half, slice_rows, LANES), f32),
            pltpu.VMEM((half, slice_rows, LANES), bf16),
            pltpu.VMEM((half, slice_rows, LANES), bf16),
            pltpu.VMEM((half, slice_rows, LANES), f32),
            pltpu.VMEM((slice_rows, LANES), f32),
            pltpu.VMEM((slice_rows // 2, LANES), f32),
            pltpu.VMEM((slice_rows // 2, LANES), f32),
            pltpu.VMEM((slice_rows // 2, LANES), f32),
            pltpu.VMEM((slice_rows // 2, LANES), f32),
            dma((2,)),
            dma((chips,)),
            dma((chips,)),
            dma((chips, half)),
            dma((chips, half)),
            dma((half,)),
            dma((half,)),
            dma((4,)),
            dma((half,)),
            dma((chips,)),
            dma((2 * half,)),
            dma((2 * half,)),
        ],
        compiler_params=pltpu.CompilerParams(collective_id=0, has_side_effects=True),
    )(slot_epoch, epoch_time, velocity, epoch_maps)
    return (both[:1], both[1])


def fits(n, epoch_maps, velocity, epochs):
    count, rows, cols = epoch_maps.shape
    chips = n // 2
    blocks = cols // LANES
    return (
        n % 8 == 0
        and velocity.shape[0] == 1
        and n * count == 2 * epochs
        and cols % LANES == 0
        and chips // 2 % blocks == 0
        and rows % (chips // 2 // blocks * 16) == 0
        and rows * cols * count <= FIT_PIXELS
    )


def local(n, epoch_maps, velocity, slot_epoch, epoch_time):
    count, rows, cols = epoch_maps.shape
    epochs = slot_epoch.shape[0]
    if fits(n, epoch_maps, velocity, epochs):
        return fused(n, epoch_maps, velocity, slot_epoch, epoch_time)
    me = lax.axis_index("vel")
    vels = lax.all_gather(velocity, "vel", axis=0, tiled=True)
    first = lax.rem(me * count, epochs)
    slots = lax.dynamic_slice_in_dim(slot_epoch, first, count, 0)
    times = epoch_time[slots]
    partial = pl.pallas_call(
        functools.partial(stack_kernel, count, rows, cols),
        out_shape=jax.ShapeDtypeStruct((vels.shape[0], rows, cols), jnp.bfloat16),
        in_specs=[
            pl.BlockSpec(memory_space=pltpu.SMEM),
            pl.BlockSpec(memory_space=pltpu.SMEM),
            pl.BlockSpec(memory_space=pltpu.VMEM),
        ],
        out_specs=pl.BlockSpec(memory_space=pltpu.VMEM),
        scratch_shapes=[
            pltpu.VMEM((count, rows, cols + 2 * HALO), jnp.bfloat16),
            pltpu.VMEM((count * 2 * LANES, LANES), jnp.bfloat16),
            pltpu.VMEM((count, rows, cols + 2 * HALO), jnp.bfloat16),
        ],
    )(vels, times, epoch_maps)
    mine = velocity.shape[0]
    received = lax.all_to_all(partial, "vel", 0, 0, tiled=True)
    received = received.reshape(2, n // 2, mine, rows, cols)
    stack_sums = jnp.sum(received.astype(jnp.float32), axis=1) / spline_norm
    likelihood = stack_sums[0] / jnp.sqrt(stack_sums[1] + 1.0)
    best_value = lax.pmax(jnp.max(likelihood, axis=0), "vel")
    return (likelihood, best_value)


def solution(mesh):
    return jax.shard_map(
        functools.partial(local, mesh.shape["vel"]),
        mesh=mesh,
        in_specs=(P("vel", "groups", None), P("vel", None), P(), P()),
        out_specs=(P("vel", "groups", None), P("groups", None)),
        check_vma=False,
    )
```

```python
import functools
import math

import jax
import jax.numpy as jnp
from jax import lax
from jax.experimental import pallas as pl
from jax.experimental.pallas import tpu as pltpu
from jax.sharding import PartitionSpec as P

SPLINE = (
    (64.0, 256.0, 64.0, 0.0),
    (27.0, 235.0, 121.0, 1.0),
    (8.0, 184.0, 184.0, 8.0),
    (1.0, 121.0, 235.0, 27.0),
)
spline_norm = 147456.0
rate_divisor = 32
HALO = 64
LANES = 128
REACH = 16
EDGE = 8
FIT_PIXELS = 1 << 19
FORWARD_LAG = 4


def scalar_taps(offset):
    whole = offset >> 2
    fraction = offset & 3
    taps = []
    for tap in range(4):
        value = jnp.float32(SPLINE[3][tap])
        for level in range(3):
            value = jnp.where(fraction == level, jnp.float32(SPLINE[level][tap]), value)
        taps.append(value)
    return whole, taps


def band(distance, offset):
    whole, taps = scalar_taps(offset)
    relative = distance - whole
    out = jnp.where(relative == 3, taps[3], 0.0)
    for tap in (2, 1, 0):
        out = jnp.where(relative == tap, taps[tap], out)
    return out.astype(jnp.bfloat16)


def stack_one(rate_row, rate_col, times, padded, bands, rows_done, count, rows, cols):
    blocks = cols // LANES
    row_distance = (
        lax.broadcasted_iota(jnp.int32, (rows, rows), 1)
        - lax.broadcasted_iota(jnp.int32, (rows, rows), 0)
        + 1
    )
    col_distance = (
        lax.broadcasted_iota(jnp.int32, (2 * LANES, LANES), 0)
        - lax.broadcasted_iota(jnp.int32, (2 * LANES, LANES), 1)
        + (1 - HALO)
    )
    for s in range(count):
        row_band = band(row_distance, (rate_row * times(s)) >> 5)
        bands[pl.ds(s * 2 * LANES, 2 * LANES), :] = band(
            col_distance, (rate_col * times(s)) >> 5
        )
        rows_done[s] = jnp.dot(
            row_band, padded[s], preferred_element_type=jnp.float32
        ).astype(jnp.bfloat16)
    lhs = jnp.concatenate(
        [
            jnp.concatenate(
                [rows_done[s, :, b * LANES : (b + 2) * LANES] for s in range(count)], axis=1
            )
            for b in range(blocks)
        ],
        axis=0,
    )
    return jnp.dot(lhs, bands[...], preferred_element_type=jnp.float32)


def pad_images(images, padded, start, count):
    zeros = jnp.zeros((images.shape[1], HALO), jnp.bfloat16)
    for s in range(count):
        padded[start + s] = jnp.concatenate([zeros, images[s], zeros], axis=1)


def stack_kernel(count, rows, cols, vel_ref, time_ref, images, out, padded, bands, rows_done):
    pad_images(images, padded, 0, count)
    hypotheses = out.shape[0]

    @pl.loop(0, hypotheses)
    def _(v):
        total = stack_one(
            vel_ref[v, 0],
            vel_ref[v, 1],
            lambda s: time_ref[s],
            padded,
            bands,
            rows_done,
            count,
            rows,
            cols,
        )
        for b in range(cols // LANES):
            out[v, :, b * LANES : (b + 1) * LANES] = total[b * rows : (b + 1) * rows].astype(
                out.dtype
            )


def tap_select(relative, taps):
    out = jnp.zeros(relative.shape, jnp.float32)
    for tap in range(4):
        if taps[tap]:
            out = jnp.where(relative == tap, jnp.float32(taps[tap]), out)
    return out


def fused_kernel(
    chips,
    epochs,
    count,
    rows,
    cols,
    se_in,
    et_in,
    vel_in,
    maps,
    out_ref,
    se_ref,
    et_ref,
    vel_ref,
    images,
    peer_images,
    row_taps,
    table,
    base,
    lhs,
    bands,
    vel_all,
    part_send,
    part_recv,
    own,
    far_send,
    far_recv,
    like_send,
    best_mine,
    max_recv,
    cross_send,
    cross_recv,
    best_send,
    load_sems,
    own_sems,
    swap_ssem,
    swap_rsem,
    vel_send,
    vel_recv,
    part_ssem,
    part_rsem,
    far_ssem,
    far_rsem,
    max_sems,
    like_ssem,
    like_rsem,
    best_ssem,
    best_rsem,
):
    like_out, best_out = out_ref.at[pl.ds(0, 1)], out_ref.at[1]
    me = lax.axis_index("vel")
    chip, core = me // 2, me % 2
    sibling = chip * 2 + 1 - core
    blocks = cols // LANES
    near_levels = chips // 4
    half = chips // 2
    slice_rows = rows * blocks // half
    share_rows = slice_rows // 2
    near0 = chip // half * half
    far0 = half - near0
    place = chip - near0
    images_all = 2 * count

    def slot(owner):
        return owner % 2 * near_levels + owner // 2 % near_levels

    def window(owner, begin, size):
        at = slot(owner)
        start = at // blocks * slice_rows + begin
        return (
            pl.ds(pl.multiple_of(start, share_rows), size),
            pl.ds(pl.multiple_of(at % blocks * LANES, LANES), LANES),
        )

    def remote(source, target, send, receive, device):
        return pltpu.make_async_remote_copy(
            src_ref=source,
            dst_ref=target,
            send_sem=send,
            recv_sem=receive,
            device_id={"vel": device},
            device_id_type=pl.DeviceIdType.MESH,
        )

    def rail(other):
        return other * 2 + core

    def each_rail(body):
        @pl.loop(1, chips)
        def _(step):
            body(lax.rem(chip + step, chips))

    def each_near(body):
        @pl.loop(1, half)
        def _(step):
            body(near0 + lax.rem(chip - near0 + step, half))

    def greet(device):
        pl.semaphore_signal(
            barrier, inc=1, device_id={"vel": device}, device_id_type=pl.DeviceIdType.MESH
        )

    early = count // 2
    loads = [
        pltpu.make_async_copy(maps.at[pl.ds(0, early)], images.at[pl.ds(0, early)], load_sems.at[0]),
        pltpu.make_async_copy(
            maps.at[pl.ds(early, count - early)], images.at[pl.ds(early, count - early)], load_sems.at[1]
        ),
        pltpu.make_async_copy(vel_in, vel_ref, load_sems.at[2]),
        pltpu.make_async_copy(se_in, se_ref, load_sems.at[3]),
        pltpu.make_async_copy(et_in, et_ref, load_sems.at[4]),
    ]
    barrier = pltpu.get_barrier_semaphore()
    greet(sibling)
    each_rail(lambda other: greet(rail(other)))
    each_near(lambda other: greet(other * 2 + 1 - core))
    for load in loads:
        load.start()

    span = rows + 2 * EDGE
    relative = (
        lax.broadcasted_iota(jnp.int32, (span, rows), 1)
        - lax.broadcasted_iota(jnp.int32, (span, rows), 0)
        + (EDGE + 1)
    )
    for f in range(4):
        row_taps[f * span : (f + 1) * span, :] = tap_select(relative, SPLINE[f]).astype(jnp.bfloat16)
    base_shape = base.shape[2:]
    for h in range(2):
        distance = (
            lax.broadcasted_iota(jnp.int32, base_shape, 0)
            - lax.broadcasted_iota(jnp.int32, base_shape, 1)
            + (HALO + 1 - REACH - h * LANES)
        )
        for f in range(4):
            base[f, h] = tap_select(distance, SPLINE[f])
    blank = jnp.zeros((blocks, REACH - EDGE, LANES), jnp.float32)

    def filter_rows(source, s, index):
        mixed = jnp.dot(row_taps[...], source[s], preferred_element_type=jnp.float32)
        mixed = mixed.astype(jnp.bfloat16).astype(jnp.float32)
        for f in range(4):
            table[index * 4 + f, :, 0 : REACH - EDGE] = blank
            table[index * 4 + f, :, REACH + rows + EDGE : rows + 2 * REACH] = blank
            for b in range(blocks):
                table[index * 4 + f, b, REACH - EDGE : REACH + rows + EDGE] = mixed[
                    f * span : (f + 1) * span, b * LANES : (b + 1) * LANES
                ]

    loads[0].wait()

    @pl.loop(0, early)
    def _(s):
        filter_rows(images, s, s)

    best_mine[...] = jnp.full_like(best_mine, -jnp.inf)
    for load in loads[1:]:
        load.wait()
    pl.semaphore_wait(barrier, chips + half - 1)

    def vel_copy(source, target, other):
        return remote(vel_ref, vel_all.at[target], vel_send.at[source], vel_recv.at[target], rail(other))

    def swap(s):
        return remote(images.at[s], peer_images.at[s], swap_ssem.at[s], swap_rsem.at[s], sibling)

    @pl.loop(0, count)
    def _(s):
        swap(s).start()

    each_rail(lambda other: vel_copy(other, chip, other).start())
    vel_all[chip, 0, 0] = vel_ref[0, 0]
    vel_all[chip, 0, 1] = vel_ref[0, 1]

    @pl.loop(early, count)
    def _(s):
        filter_rows(images, s, s)

    @pl.loop(0, count)
    def _(s):
        swap(s).wait_recv()
        filter_rows(peer_images, s, s + count)

    first = lax.rem(me * count, epochs)
    peer_first = lax.rem(sibling * count, epochs)

    def time(s):
        at = first + s if s < count else peer_first + (s - count)
        return et_ref[se_ref[at]]

    def stack(rate_row, rate_col):
        for s in range(images_all):
            qr = (rate_row * time(s)) >> 5
            qc = (rate_col * time(s)) >> 5
            for b in range(blocks):
                lhs[b * rows : (b + 1) * rows, s * LANES : (s + 1) * LANES] = table[
                    s * 4 + (qr & 3), b, pl.ds((qr >> 2) + REACH, rows), :
                ].astype(jnp.bfloat16)
            for h in range(2):
                bands[s * LANES : (s + 1) * LANES, h * LANES : (h + 1) * LANES] = base[
                    qc & 3, h, pl.ds(REACH - (qc >> 2), LANES), :
                ].astype(jnp.bfloat16)
        wide = jnp.dot(lhs[...], bands[...], preferred_element_type=jnp.float32)
        tiles = []
        for t in range(blocks + 1):
            tile = None
            if t < blocks:
                tile = wide[t * rows : (t + 1) * rows, :LANES]
            if t:
                right = wide[(t - 1) * rows : t * rows, LANES:]
                tile = right if tile is None else tile + right
            tiles.append(pltpu.roll(tile, HALO, 1))
        left = lax.broadcasted_iota(jnp.int32, (rows, LANES), 1) < HALO
        return [jnp.where(left, tiles[b], tiles[b + 1]) for b in range(blocks)]

    def part_copy(v, source, other):
        return remote(
            part_send.at[v, slot(other)],
            part_recv.at[v, source - near0],
            part_ssem.at[v, other - near0],
            part_rsem.at[v, source - near0],
            rail(other),
        )

    def far_copy(f):
        return remote(
            far_send.at[f], far_recv.at[f], far_ssem.at[f], far_rsem.at[f], rail(far0 + place)
        )

    def like_copy(o, owner):
        where = window(owner, 0, slice_rows)
        return remote(
            like_send.at[o],
            like_out.at[0, where[0], where[1]],
            like_ssem.at[o],
            like_rsem.at[owner],
            rail(near0 + o),
        )

    def near_sum(v):
        each_near(lambda other: part_copy(v, other, other).wait_recv())
        total = own[v, slot(chip)]
        for step in range(1, half):
            total = total + part_recv[v, lax.rem(place + step, half)].astype(jnp.float32)
        return total

    def forward(f):
        far_send[f] = near_sum(far0 + f).astype(jnp.bfloat16)
        far_copy(f).start()

    def finish_like(o):
        near = near_sum(near0 + o)
        far_copy(o).wait_recv()
        far = far_recv[o].astype(jnp.float32)
        first_kind = near0 == 0
        signal = jnp.where(first_kind, near, far) / spline_norm
        weight = jnp.where(first_kind, far, near) / spline_norm
        value = signal / jnp.sqrt(weight + 1.0)
        best_mine[...] = jnp.maximum(best_mine[...], value)
        like_send[o] = value

    @pl.loop(0, chips)
    def _(i):
        begun = (i + chips - 1) // chips
        later = (i - 1 - half + chips) // chips
        turn = (i - 1 - half) * later
        near_v = near0 + (turn + (turn - place + half) // half) * later + place * (1 - begun)
        is_far = begun - later
        v = is_far * (far0 + i - 1) + (1 - is_far) * near_v

        @pl.when(i >= 1)
        def _():
            vel_copy(v, v, v).wait_recv()

        total = stack(vel_all[v, 0, 0], vel_all[v, 0, 1])
        for at in range(half):
            start = at // blocks * slice_rows
            piece = total[at % blocks][start : start + slice_rows]
            own[v, at] = piece
            part_send[v, at] = piece.astype(jnp.bfloat16)

        each_near(lambda other: part_copy(v, chip, other).start())

        @pl.when(i >= 1 + FORWARD_LAG)
        def _():
            forward(i - 1 - FORWARD_LAG)

    @pl.loop(chips - 1 - FORWARD_LAG, half)
    def _(f):
        forward(f)

    @pl.loop(0, half)
    def _(o):
        finish_like(o)

    other_core = 1 - core
    mine = pl.ds(pl.multiple_of(core * share_rows, share_rows), share_rows)
    theirs = pl.ds(pl.multiple_of(other_core * share_rows, share_rows), share_rows)
    meet = remote(best_mine.at[theirs], max_recv, max_sems.at[0], max_sems.at[1], sibling)
    meet.start()
    meet.wait_recv()
    cross_send[...] = jnp.maximum(best_mine[mine, :], max_recv[...])
    cross = remote(cross_send, cross_recv, max_sems.at[2], max_sems.at[3], rail(far0 + place))
    cross.start()
    each_near(lambda other: like_copy(other - near0, chip).start())
    where = window(chip, 0, slice_rows)
    keeps = [
        pltpu.make_async_copy(
            like_send.at[place], like_out.at[0, where[0], where[1]], own_sems.at[0]
        )
    ]
    keeps[0].start()
    cross.wait_recv()
    best_send[...] = jnp.maximum(cross_send[...], cross_recv[...])

    def best_copy(source, target):
        where = window(source // 2, source % 2 * share_rows, share_rows)
        return remote(
            best_send,
            best_out.at[where[0], where[1]],
            best_ssem.at[target],
            best_rsem.at[source],
            near0 * 2 + target,
        )

    seat = place * 2 + core

    def each_seat(body):
        @pl.loop(1, 2 * half)
        def _(step):
            body(lax.rem(seat + step, 2 * half))

    each_seat(lambda target: best_copy(seat, target).start())
    where = window(chip, core * share_rows, share_rows)
    keeps.append(
        pltpu.make_async_copy(best_send, best_out.at[where[0], where[1]], own_sems.at[1])
    )
    keeps[1].start()

    @pl.loop(0, chips)
    def _(v):
        each_near(lambda other: part_copy(v, chip, other).wait_send())

    @pl.loop(0, half)
    def _(f):
        far_copy(f).wait_send()

    @pl.loop(0, count)
    def _(s):
        swap(s).wait_send()

    for keep in keeps:
        keep.wait()
    meet.wait_send()
    cross.wait_send()
    each_rail(lambda other: vel_copy(other, chip, other).wait_send())
    each_near(lambda other: like_copy(other - near0, other).wait())
    each_seat(lambda other: best_copy(other, other).wait())


def fused(n, epoch_maps, velocity, slot_epoch, epoch_time):
    count, rows, cols = epoch_maps.shape
    epochs = slot_epoch.shape[0]
    chips = n // 2
    half = chips // 2
    blocks = cols // LANES
    slice_rows = rows * blocks // half
    whole = pl.BlockSpec(memory_space=pl.ANY)
    f32, bf16 = jnp.float32, jnp.bfloat16
    dma = pltpu.SemaphoreType.DMA
    both = pl.pallas_call(
        functools.partial(fused_kernel, chips, epochs, count, rows, cols),
        out_shape=jax.ShapeDtypeStruct((2, rows, cols), f32),
        in_specs=[whole] * 4,
        out_specs=whole,
        scratch_shapes=[
            pltpu.SMEM((epochs,), jnp.int32),
            pltpu.SMEM((epochs,), jnp.int32),
            pltpu.SMEM((1, 2), jnp.int32),
            pltpu.VMEM((count, rows, cols), bf16),
            pltpu.VMEM((count, rows, cols), bf16),
            pltpu.VMEM((4 * (rows + 2 * EDGE), rows), bf16),
            pltpu.VMEM((2 * count * 4, blocks, rows + 2 * REACH, LANES), f32),
            pltpu.VMEM((4, 2, LANES + 2 * REACH, LANES), f32),
            pltpu.VMEM((blocks * rows, 2 * count * LANES), bf16),
            pltpu.VMEM((2 * count * LANES, 2 * LANES), bf16),
            pltpu.SMEM((chips, 1, 2), jnp.int32),
            pltpu.VMEM((chips, half, slice_rows, LANES), bf16),
            pltpu.VMEM((chips, half, slice_rows, LANES), bf16),
            pltpu.VMEM((chips, half, slice_rows, LANES), f32),
            pltpu.VMEM((half, slice_rows, LANES), bf16),
            pltpu.VMEM((half, slice_rows, LANES), bf16),
            pltpu.VMEM((half, slice_rows, LANES), f32),
            pltpu.VMEM((slice_rows, LANES), f32),
            pltpu.VMEM((slice_rows // 2, LANES), f32),
            pltpu.VMEM((slice_rows // 2, LANES), f32),
            pltpu.VMEM((slice_rows // 2, LANES), f32),
            pltpu.VMEM((slice_rows // 2, LANES), f32),
            dma((5,)),
            dma((2,)),
            dma((count,)),
            dma((count,)),
            dma((chips,)),
            dma((chips,)),
            dma((chips, half)),
            dma((chips, half)),
            dma((half,)),
            dma((half,)),
            dma((4,)),
            dma((half,)),
            dma((chips,)),
            dma((2 * half,)),
            dma((2 * half,)),
        ],
        compiler_params=pltpu.CompilerParams(collective_id=0, has_side_effects=True),
    )(slot_epoch, epoch_time, velocity, epoch_maps)
    return (both[:1], both[1])


def fits(n, epoch_maps, velocity, epochs):
    count, rows, cols = epoch_maps.shape
    chips = n // 2
    blocks = cols // LANES
    return (
        n % 8 == 0
        and velocity.shape[0] == 1
        and n * count == 2 * epochs
        and cols % LANES == 0
        and chips // 2 % blocks == 0
        and rows % (chips // 2 // blocks * 16) == 0
        and rows * cols * count <= FIT_PIXELS
    )


def local(n, epoch_maps, velocity, slot_epoch, epoch_time):
    count, rows, cols = epoch_maps.shape
    epochs = slot_epoch.shape[0]
    if fits(n, epoch_maps, velocity, epochs):
        return fused(n, epoch_maps, velocity, slot_epoch, epoch_time)
    me = lax.axis_index("vel")
    vels = lax.all_gather(velocity, "vel", axis=0, tiled=True)
    first = lax.rem(me * count, epochs)
    slots = lax.dynamic_slice_in_dim(slot_epoch, first, count, 0)
    times = epoch_time[slots]
    partial = pl.pallas_call(
        functools.partial(stack_kernel, count, rows, cols),
        out_shape=jax.ShapeDtypeStruct((vels.shape[0], rows, cols), jnp.bfloat16),
        in_specs=[
            pl.BlockSpec(memory_space=pltpu.SMEM),
            pl.BlockSpec(memory_space=pltpu.SMEM),
            pl.BlockSpec(memory_space=pltpu.VMEM),
        ],
        out_specs=pl.BlockSpec(memory_space=pltpu.VMEM),
        scratch_shapes=[
            pltpu.VMEM((count, rows, cols + 2 * HALO), jnp.bfloat16),
            pltpu.VMEM((count * 2 * LANES, LANES), jnp.bfloat16),
            pltpu.VMEM((count, rows, cols + 2 * HALO), jnp.bfloat16),
        ],
    )(vels, times, epoch_maps)
    mine = velocity.shape[0]
    received = lax.all_to_all(partial, "vel", 0, 0, tiled=True)
    received = received.reshape(2, n // 2, mine, rows, cols)
    stack_sums = jnp.sum(received.astype(jnp.float32), axis=1) / spline_norm
    likelihood = stack_sums[0] / jnp.sqrt(stack_sums[1] + 1.0)
    best_value = lax.pmax(jnp.max(likelihood, axis=0), "vel")
    return (likelihood, best_value)


def solution(mesh):
    return jax.shard_map(
        functools.partial(local, mesh.shape["vel"]),
        mesh=mesh,
        in_specs=(P("vel", "groups", None), P("vel", None), P(), P()),
        out_specs=(P("vel", "groups", None), P("groups", None)),
        check_vma=False,
    )
```

```python
import functools
import math

import jax
import jax.numpy as jnp
from jax import lax
from jax.experimental import pallas as pl
from jax.experimental.pallas import tpu as pltpu
from jax.sharding import PartitionSpec as P

SPLINE = (
    (64.0, 256.0, 64.0, 0.0),
    (27.0, 235.0, 121.0, 1.0),
    (8.0, 184.0, 184.0, 8.0),
    (1.0, 121.0, 235.0, 27.0),
)
spline_norm = 147456.0
rate_divisor = 32
HALO = 64
LANES = 128
REACH = 16
EDGE = 8
FIT_PIXELS = 1 << 19
FORWARD_LAG = 4


def scalar_taps(offset):
    whole = offset >> 2
    fraction = offset & 3
    taps = []
    for tap in range(4):
        value = jnp.float32(SPLINE[3][tap])
        for level in range(3):
            value = jnp.where(fraction == level, jnp.float32(SPLINE[level][tap]), value)
        taps.append(value)
    return whole, taps


def band(distance, offset):
    whole, taps = scalar_taps(offset)
    relative = distance - whole
    out = jnp.where(relative == 3, taps[3], 0.0)
    for tap in (2, 1, 0):
        out = jnp.where(relative == tap, taps[tap], out)
    return out.astype(jnp.bfloat16)


def stack_one(rate_row, rate_col, times, padded, bands, rows_done, count, rows, cols):
    blocks = cols // LANES
    row_distance = (
        lax.broadcasted_iota(jnp.int32, (rows, rows), 1)
        - lax.broadcasted_iota(jnp.int32, (rows, rows), 0)
        + 1
    )
    col_distance = (
        lax.broadcasted_iota(jnp.int32, (2 * LANES, LANES), 0)
        - lax.broadcasted_iota(jnp.int32, (2 * LANES, LANES), 1)
        + (1 - HALO)
    )
    for s in range(count):
        row_band = band(row_distance, (rate_row * times(s)) >> 5)
        bands[pl.ds(s * 2 * LANES, 2 * LANES), :] = band(
            col_distance, (rate_col * times(s)) >> 5
        )
        rows_done[s] = jnp.dot(
            row_band, padded[s], preferred_element_type=jnp.float32
        ).astype(jnp.bfloat16)
    lhs = jnp.concatenate(
        [
            jnp.concatenate(
                [rows_done[s, :, b * LANES : (b + 2) * LANES] for s in range(count)], axis=1
            )
            for b in range(blocks)
        ],
        axis=0,
    )
    return jnp.dot(lhs, bands[...], preferred_element_type=jnp.float32)


def pad_images(images, padded, start, count):
    zeros = jnp.zeros((images.shape[1], HALO), jnp.bfloat16)
    for s in range(count):
        padded[start + s] = jnp.concatenate([zeros, images[s], zeros], axis=1)


def stack_kernel(count, rows, cols, vel_ref, time_ref, images, out, padded, bands, rows_done):
    pad_images(images, padded, 0, count)
    hypotheses = out.shape[0]

    @pl.loop(0, hypotheses)
    def _(v):
        total = stack_one(
            vel_ref[v, 0],
            vel_ref[v, 1],
            lambda s: time_ref[s],
            padded,
            bands,
            rows_done,
            count,
            rows,
            cols,
        )
        for b in range(cols // LANES):
            out[v, :, b * LANES : (b + 1) * LANES] = total[b * rows : (b + 1) * rows].astype(
                out.dtype
            )


def tap_select(relative, taps):
    out = jnp.zeros(relative.shape, jnp.float32)
    for tap in range(4):
        if taps[tap]:
            out = jnp.where(relative == tap, jnp.float32(taps[tap]), out)
    return out


def fused_kernel(
    chips,
    epochs,
    count,
    rows,
    cols,
    se_in,
    et_in,
    vel_in,
    maps,
    out_ref,
    se_ref,
    et_ref,
    vel_ref,
    images,
    peer_images,
    row_taps,
    table,
    base,
    vel_all,
    part_send,
    part_recv,
    own,
    far_send,
    far_recv,
    like_send,
    best_mine,
    meet_recv,
    best_send,
    load_sems,
    own_sems,
    swap_ssem,
    swap_rsem,
    vel_send,
    vel_recv,
    part_ssem,
    part_rsem,
    far_ssem,
    far_rsem,
    meet_ssem,
    meet_rsem,
    like_ssem,
    like_rsem,
    best_ssem,
    best_rsem,
):
    like_out, best_out = out_ref.at[pl.ds(0, 1)], out_ref.at[1]
    me = lax.axis_index("vel")
    chip, core = me // 2, me % 2
    sibling = chip * 2 + 1 - core
    blocks = cols // LANES
    near_levels = chips // 4
    half = chips // 2
    slice_rows = rows * blocks // half
    share_rows = slice_rows // 2
    near0 = chip // half * half
    far0 = half - near0
    place = chip - near0
    images_all = 2 * count

    def slot(owner):
        return owner % 2 * near_levels + owner // 2 % near_levels

    def window(owner, begin, size):
        at = slot(owner)
        start = at // blocks * slice_rows + begin
        return (
            pl.ds(pl.multiple_of(start, share_rows), size),
            pl.ds(pl.multiple_of(at % blocks * LANES, LANES), LANES),
        )

    def remote(source, target, send, receive, device):
        return pltpu.make_async_remote_copy(
            src_ref=source,
            dst_ref=target,
            send_sem=send,
            recv_sem=receive,
            device_id={"vel": device},
            device_id_type=pl.DeviceIdType.MESH,
        )

    def rail(other):
        return other * 2 + core

    def each_rail(body):
        @pl.loop(1, chips)
        def _(step):
            body(lax.rem(chip + step, chips))

    def each_near(body):
        @pl.loop(1, half)
        def _(step):
            body(near0 + lax.rem(chip - near0 + step, half))

    def greet(device):
        pl.semaphore_signal(
            barrier, inc=1, device_id={"vel": device}, device_id_type=pl.DeviceIdType.MESH
        )

    early = count // 2
    loads = [
        pltpu.make_async_copy(maps.at[pl.ds(0, early)], images.at[pl.ds(0, early)], load_sems.at[0]),
        pltpu.make_async_copy(
            maps.at[pl.ds(early, count - early)], images.at[pl.ds(early, count - early)], load_sems.at[1]
        ),
        pltpu.make_async_copy(vel_in, vel_ref, load_sems.at[2]),
        pltpu.make_async_copy(se_in, se_ref, load_sems.at[3]),
        pltpu.make_async_copy(et_in, et_ref, load_sems.at[4]),
    ]
    barrier = pltpu.get_barrier_semaphore()
    greet(sibling)
    each_rail(lambda other: greet(rail(other)))
    each_near(lambda other: greet(other * 2 + 1 - core))
    greet((far0 + place) * 2 + 1 - core)
    for load in loads:
        load.start()

    span = rows + 2 * EDGE
    relative = (
        lax.broadcasted_iota(jnp.int32, (span, rows), 1)
        - lax.broadcasted_iota(jnp.int32, (span, rows), 0)
        + (EDGE + 1)
    )
    for f in range(4):
        row_taps[f * span : (f + 1) * span, :] = tap_select(relative, SPLINE[f]).astype(jnp.bfloat16)
    base_shape = base.shape[2:]
    for h in range(2):
        distance = (
            lax.broadcasted_iota(jnp.int32, base_shape, 0)
            - lax.broadcasted_iota(jnp.int32, base_shape, 1)
            + (HALO + 1 - REACH - h * LANES)
        )
        for f in range(4):
            base[f, h] = tap_select(distance, SPLINE[f])
    blank = jnp.zeros((blocks, REACH - EDGE, LANES), jnp.float32)

    def filter_rows(source, s, index):
        mixed = jnp.dot(row_taps[...], source[s], preferred_element_type=jnp.float32)
        mixed = mixed.astype(jnp.bfloat16).astype(jnp.float32)
        for f in range(4):
            table[index * 4 + f, :, 0 : REACH - EDGE] = blank
            table[index * 4 + f, :, REACH + rows + EDGE : rows + 2 * REACH] = blank
            for b in range(blocks):
                table[index * 4 + f, b, REACH - EDGE : REACH + rows + EDGE] = mixed[
                    f * span : (f + 1) * span, b * LANES : (b + 1) * LANES
                ]

    loads[0].wait()

    @pl.loop(0, early, step=2)
    def _(s):
        filter_rows(images, s, s)
        filter_rows(images, s + 1, s + 1)

    best_mine[...] = jnp.full_like(best_mine, -jnp.inf)
    for load in loads[1:]:
        load.wait()
    pl.semaphore_wait(barrier, chips + half)

    def vel_copy(source, target, other):
        return remote(vel_ref, vel_all.at[target], vel_send.at[source], vel_recv.at[target], rail(other))

    def swap(s):
        return remote(images.at[s], peer_images.at[s], swap_ssem.at[s], swap_rsem.at[s], sibling)

    @pl.loop(0, count)
    def _(s):
        swap(s).start()

    each_rail(lambda other: vel_copy(other, chip, other).start())
    vel_all[chip, 0, 0] = vel_ref[0, 0]
    vel_all[chip, 0, 1] = vel_ref[0, 1]

    @pl.loop(early, count, step=2)
    def _(s):
        filter_rows(images, s, s)
        filter_rows(images, s + 1, s + 1)

    @pl.loop(0, count, step=2)
    def _(s):
        swap(s).wait_recv()
        swap(s + 1).wait_recv()
        filter_rows(peer_images, s, s + count)
        filter_rows(peer_images, s + 1, s + 1 + count)

    first = lax.rem(me * count, epochs)
    peer_first = lax.rem(sibling * count, epochs)

    def time(s):
        at = first + s if s < count else peer_first + (s - count)
        return et_ref[se_ref[at]]

    def stack(rate_row, rate_col):
        shifted, weights = [], []
        for s in range(images_all):
            qr = (rate_row * time(s)) >> 5
            qc = (rate_col * time(s)) >> 5
            shifted.append([
                table[s * 4 + (qr & 3), b, pl.ds((qr >> 2) + REACH, rows), :].astype(jnp.bfloat16)
                for b in range(blocks)
            ])
            weights.append(
                jnp.concatenate(
                    [
                        base[qc & 3, h, pl.ds(REACH - (qc >> 2), LANES), :].astype(jnp.bfloat16)
                        for h in range(2)
                    ],
                    axis=1,
                )
            )
        lhs_all = jnp.concatenate(
            [
                jnp.concatenate([shifted[s][b] for s in range(images_all)], axis=1)
                for b in range(blocks)
            ],
            axis=0,
        )
        wide = jnp.dot(lhs_all, jnp.concatenate(weights, axis=0), preferred_element_type=jnp.float32)
        tiles = []
        for t in range(blocks + 1):
            tile = None
            if t < blocks:
                tile = wide[t * rows : (t + 1) * rows, :LANES]
            if t:
                right = wide[(t - 1) * rows : t * rows, LANES:]
                tile = right if tile is None else tile + right
            tiles.append(pltpu.roll(tile, HALO, 1))
        left = lax.broadcasted_iota(jnp.int32, (rows, LANES), 1) < HALO
        return [jnp.where(left, tiles[b], tiles[b + 1]) for b in range(blocks)]

    def part_copy(v, source, other):
        return remote(
            part_send.at[v, slot(other)],
            part_recv.at[v, source - near0],
            part_ssem.at[v, other - near0],
            part_rsem.at[v, source - near0],
            rail(other),
        )

    def far_copy(f):
        return remote(
            far_send.at[f], far_recv.at[f], far_ssem.at[f], far_rsem.at[f], rail(far0 + place)
        )

    def like_copy(o, owner):
        where = window(owner, 0, slice_rows)
        return remote(
            like_send.at[o],
            like_out.at[0, where[0], where[1]],
            like_ssem.at[o],
            like_rsem.at[owner],
            rail(near0 + o),
        )

    def near_sum(v):
        each_near(lambda other: part_copy(v, other, other).wait_recv())
        total = own[v, slot(chip)]
        for step in range(1, half):
            total = total + part_recv[v, lax.rem(place + step, half)].astype(jnp.float32)
        return total

    def forward(f):
        far_send[f] = near_sum(far0 + f).astype(jnp.bfloat16)
        far_copy(f).start()

    def finish_like(o):
        near = near_sum(near0 + o)
        far_copy(o).wait_recv()
        far = far_recv[o].astype(jnp.float32)
        first_kind = near0 == 0
        signal = jnp.where(first_kind, near, far) / spline_norm
        weight = jnp.where(first_kind, far, near) / spline_norm
        value = signal / jnp.sqrt(weight + 1.0)
        best_mine[...] = jnp.maximum(best_mine[...], value)
        like_send[o] = value

    @pl.loop(0, chips)
    def _(i):
        begun = (i + chips - 1) // chips
        later = (i - 1 - half + chips) // chips
        turn = (i - 1 - half) * later
        near_v = near0 + (turn + (turn - place + half) // half) * later + place * (1 - begun)
        is_far = begun - later
        v = is_far * (far0 + i - 1) + (1 - is_far) * near_v

        @pl.when(i >= 1)
        def _():
            vel_copy(v, v, v).wait_recv()

        total = stack(vel_all[v, 0, 0], vel_all[v, 0, 1])
        for at in range(half):
            start = at // blocks * slice_rows
            piece = total[at % blocks][start : start + slice_rows]
            own[v, at] = piece
            part_send[v, at] = piece.astype(jnp.bfloat16)

        each_near(lambda other: part_copy(v, chip, other).start())

        @pl.when(i >= 1 + FORWARD_LAG)
        def _():
            forward(i - 1 - FORWARD_LAG)

    @pl.loop(chips - 1 - FORWARD_LAG, half)
    def _(f):
        forward(f)

    @pl.loop(0, half)
    def _(o):
        finish_like(o)

    other_core = 1 - core
    mine = pl.ds(pl.multiple_of(core * share_rows, share_rows), share_rows)
    theirs = pl.ds(pl.multiple_of(other_core * share_rows, share_rows), share_rows)
    mirror = far0 + place
    meets = [
        remote(best_mine.at[theirs], meet_recv.at[0], meet_ssem.at[0], meet_rsem.at[0], sibling),
        remote(best_mine.at[mine], meet_recv.at[1], meet_ssem.at[1], meet_rsem.at[1], rail(mirror)),
        remote(
            best_mine.at[theirs], meet_recv.at[2], meet_ssem.at[2], meet_rsem.at[2], mirror * 2 + other_core
        ),
    ]
    for meet in (meets[1], meets[2], meets[0]):
        meet.start()
    each_near(lambda other: like_copy(other - near0, chip).start())
    where = window(chip, 0, slice_rows)
    keeps = [
        pltpu.make_async_copy(
            like_send.at[place], like_out.at[0, where[0], where[1]], own_sems.at[0]
        )
    ]
    keeps[0].start()
    for meet in meets:
        meet.wait_recv()
    best = jnp.maximum(best_mine[mine, :], meet_recv[0])
    best_send[...] = jnp.maximum(best, jnp.maximum(meet_recv[1], meet_recv[2]))

    def best_copy(source, target):
        where = window(source // 2, source % 2 * share_rows, share_rows)
        return remote(
            best_send,
            best_out.at[where[0], where[1]],
            best_ssem.at[target],
            best_rsem.at[source],
            near0 * 2 + target,
        )

    seat = place * 2 + core

    def each_seat(body):
        @pl.loop(1, 2 * half)
        def _(step):
            body(lax.rem(seat + step, 2 * half))

    each_seat(lambda target: best_copy(seat, target).start())
    where = window(chip, core * share_rows, share_rows)
    keeps.append(
        pltpu.make_async_copy(best_send, best_out.at[where[0], where[1]], own_sems.at[1])
    )
    keeps[1].start()

    @pl.loop(0, chips)
    def _(v):
        each_near(lambda other: part_copy(v, chip, other).wait_send())

    @pl.loop(0, half)
    def _(f):
        far_copy(f).wait_send()

    @pl.loop(0, count)
    def _(s):
        swap(s).wait_send()

    for keep in keeps:
        keep.wait()
    for meet in meets:
        meet.wait_send()

    each_rail(lambda other: vel_copy(other, chip, other).wait_send())
    each_near(lambda other: like_copy(other - near0, other).wait())
    each_seat(lambda other: best_copy(other, other).wait())


def fused(n, epoch_maps, velocity, slot_epoch, epoch_time):
    count, rows, cols = epoch_maps.shape
    epochs = slot_epoch.shape[0]
    chips = n // 2
    half = chips // 2
    blocks = cols // LANES
    slice_rows = rows * blocks // half
    whole = pl.BlockSpec(memory_space=pl.ANY)
    f32, bf16 = jnp.float32, jnp.bfloat16
    dma = pltpu.SemaphoreType.DMA
    both = pl.pallas_call(
        functools.partial(fused_kernel, chips, epochs, count, rows, cols),
        out_shape=jax.ShapeDtypeStruct((2, rows, cols), f32),
        in_specs=[whole] * 4,
        out_specs=whole,
        scratch_shapes=[
            pltpu.SMEM((epochs,), jnp.int32),
            pltpu.SMEM((epochs,), jnp.int32),
            pltpu.SMEM((1, 2), jnp.int32),
            pltpu.VMEM((count, rows, cols), bf16),
            pltpu.VMEM((count, rows, cols), bf16),
            pltpu.VMEM((4 * (rows + 2 * EDGE), rows), bf16),
            pltpu.VMEM((2 * count * 4, blocks, rows + 2 * REACH, LANES), f32),
            pltpu.VMEM((4, 2, LANES + 2 * REACH, LANES), f32),
            pltpu.SMEM((chips, 1, 2), jnp.int32),
            pltpu.VMEM((chips, half, slice_rows, LANES), bf16),
            pltpu.VMEM((chips, half, slice_rows, LANES), bf16),
            pltpu.VMEM((chips, half, slice_rows, LANES), f32),
            pltpu.VMEM((half, slice_rows, LANES), bf16),
            pltpu.VMEM((half, slice_rows, LANES), bf16),
            pltpu.VMEM((half, slice_rows, LANES), f32),
            pltpu.VMEM((slice_rows, LANES), f32),
            pltpu.VMEM((3, slice_rows // 2, LANES), f32),
            pltpu.VMEM((slice_rows // 2, LANES), f32),
            dma((5,)),
            dma((2,)),
            dma((count,)),
            dma((count,)),
            dma((chips,)),
            dma((chips,)),
            dma((chips, half)),
            dma((chips, half)),
            dma((half,)),
            dma((half,)),
            dma((3,)),
            dma((3,)),
            dma((half,)),
            dma((chips,)),
            dma((2 * half,)),
            dma((2 * half,)),
        ],
        compiler_params=pltpu.CompilerParams(collective_id=0, has_side_effects=True),
    )(slot_epoch, epoch_time, velocity, epoch_maps)
    return (both[:1], both[1])


def fits(n, epoch_maps, velocity, epochs):
    count, rows, cols = epoch_maps.shape
    chips = n // 2
    blocks = cols // LANES
    return (
        n % 8 == 0
        and count % 4 == 0
        and velocity.shape[0] == 1
        and n * count == 2 * epochs
        and cols % LANES == 0
        and chips // 2 % blocks == 0
        and rows % (chips // 2 // blocks * 16) == 0
        and rows * cols * count <= FIT_PIXELS
    )


def local(n, epoch_maps, velocity, slot_epoch, epoch_time):
    count, rows, cols = epoch_maps.shape
    epochs = slot_epoch.shape[0]
    if fits(n, epoch_maps, velocity, epochs):
        return fused(n, epoch_maps, velocity, slot_epoch, epoch_time)
    me = lax.axis_index("vel")
    vels = lax.all_gather(velocity, "vel", axis=0, tiled=True)
    first = lax.rem(me * count, epochs)
    slots = lax.dynamic_slice_in_dim(slot_epoch, first, count, 0)
    times = epoch_time[slots]
    partial = pl.pallas_call(
        functools.partial(stack_kernel, count, rows, cols),
        out_shape=jax.ShapeDtypeStruct((vels.shape[0], rows, cols), jnp.bfloat16),
        in_specs=[
            pl.BlockSpec(memory_space=pltpu.SMEM),
            pl.BlockSpec(memory_space=pltpu.SMEM),
            pl.BlockSpec(memory_space=pltpu.VMEM),
        ],
        out_specs=pl.BlockSpec(memory_space=pltpu.VMEM),
        scratch_shapes=[
            pltpu.VMEM((count, rows, cols + 2 * HALO), jnp.bfloat16),
            pltpu.VMEM((count * 2 * LANES, LANES), jnp.bfloat16),
            pltpu.VMEM((count, rows, cols + 2 * HALO), jnp.bfloat16),
        ],
    )(vels, times, epoch_maps)
    mine = velocity.shape[0]
    received = lax.all_to_all(partial, "vel", 0, 0, tiled=True)
    received = received.reshape(2, n // 2, mine, rows, cols)
    stack_sums = jnp.sum(received.astype(jnp.float32), axis=1) / spline_norm
    likelihood = stack_sums[0] / jnp.sqrt(stack_sums[1] + 1.0)
    best_value = lax.pmax(jnp.max(likelihood, axis=0), "vel")
    return (likelihood, best_value)


def solution(mesh):
    return jax.shard_map(
        functools.partial(local, mesh.shape["vel"]),
        mesh=mesh,
        in_specs=(P("vel", "groups", None), P("vel", None), P(), P()),
        out_specs=(P("vel", "groups", None), P("groups", None)),
        check_vma=False,
    )
```

```python
import functools
import math

import jax
import jax.numpy as jnp
from jax import lax
from jax.experimental import pallas as pl
from jax.experimental.pallas import tpu as pltpu
from jax.sharding import PartitionSpec as P

SPLINE = (
    (64.0, 256.0, 64.0, 0.0),
    (27.0, 235.0, 121.0, 1.0),
    (8.0, 184.0, 184.0, 8.0),
    (1.0, 121.0, 235.0, 27.0),
)
spline_norm = 147456.0
rate_divisor = 32
HALO = 64
LANES = 128
REACH = 16
EDGE = 8
FIT_PIXELS = 1 << 19
FORWARD_LAG = 4


def scalar_taps(offset):
    whole = offset >> 2
    fraction = offset & 3
    taps = []
    for tap in range(4):
        value = jnp.float32(SPLINE[3][tap])
        for level in range(3):
            value = jnp.where(fraction == level, jnp.float32(SPLINE[level][tap]), value)
        taps.append(value)
    return whole, taps


def band(distance, offset):
    whole, taps = scalar_taps(offset)
    relative = distance - whole
    out = jnp.where(relative == 3, taps[3], 0.0)
    for tap in (2, 1, 0):
        out = jnp.where(relative == tap, taps[tap], out)
    return out.astype(jnp.bfloat16)


def stack_one(rate_row, rate_col, times, padded, bands, rows_done, count, rows, cols):
    blocks = cols // LANES
    row_distance = (
        lax.broadcasted_iota(jnp.int32, (rows, rows), 1)
        - lax.broadcasted_iota(jnp.int32, (rows, rows), 0)
        + 1
    )
    col_distance = (
        lax.broadcasted_iota(jnp.int32, (2 * LANES, LANES), 0)
        - lax.broadcasted_iota(jnp.int32, (2 * LANES, LANES), 1)
        + (1 - HALO)
    )
    for s in range(count):
        row_band = band(row_distance, (rate_row * times(s)) >> 5)
        bands[pl.ds(s * 2 * LANES, 2 * LANES), :] = band(
            col_distance, (rate_col * times(s)) >> 5
        )
        rows_done[s] = jnp.dot(
            row_band, padded[s], preferred_element_type=jnp.float32
        ).astype(jnp.bfloat16)
    lhs = jnp.concatenate(
        [
            jnp.concatenate(
                [rows_done[s, :, b * LANES : (b + 2) * LANES] for s in range(count)], axis=1
            )
            for b in range(blocks)
        ],
        axis=0,
    )
    return jnp.dot(lhs, bands[...], preferred_element_type=jnp.float32)


def pad_images(images, padded, start, count):
    zeros = jnp.zeros((images.shape[1], HALO), jnp.bfloat16)
    for s in range(count):
        padded[start + s] = jnp.concatenate([zeros, images[s], zeros], axis=1)


def stack_kernel(count, rows, cols, vel_ref, time_ref, images, out, padded, bands, rows_done):
    pad_images(images, padded, 0, count)
    hypotheses = out.shape[0]

    @pl.loop(0, hypotheses)
    def _(v):
        total = stack_one(
            vel_ref[v, 0],
            vel_ref[v, 1],
            lambda s: time_ref[s],
            padded,
            bands,
            rows_done,
            count,
            rows,
            cols,
        )
        for b in range(cols // LANES):
            out[v, :, b * LANES : (b + 1) * LANES] = total[b * rows : (b + 1) * rows].astype(
                out.dtype
            )


def tap_select(relative, taps):
    out = jnp.zeros(relative.shape, jnp.float32)
    for tap in range(4):
        if taps[tap]:
            out = jnp.where(relative == tap, jnp.float32(taps[tap]), out)
    return out


def fused_kernel(
    chips,
    epochs,
    count,
    rows,
    cols,
    se_in,
    et_in,
    vel_in,
    maps,
    out_ref,
    se_ref,
    et_ref,
    vel_ref,
    images,
    peer_images,
    row_taps,
    table,
    base,
    vel_all,
    part_send,
    part_recv,
    own,
    far_send,
    far_recv,
    like_send,
    best_mine,
    meet_recv,
    best_send,
    load_sems,
    own_sems,
    swap_ssem,
    swap_rsem,
    vel_send,
    vel_recv,
    part_ssem,
    part_rsem,
    far_ssem,
    far_rsem,
    meet_ssem,
    meet_rsem,
    like_ssem,
    like_rsem,
    best_ssem,
    best_rsem,
):
    like_out, best_out = out_ref.at[pl.ds(0, 1)], out_ref.at[1]
    me = lax.axis_index("vel")
    chip, core = me // 2, me % 2
    sibling = chip * 2 + 1 - core
    blocks = cols // LANES
    near_levels = chips // 4
    half = chips // 2
    slice_rows = rows * blocks // half
    share_rows = slice_rows // 2
    near0 = chip // half * half
    far0 = half - near0
    place = chip - near0
    images_all = 2 * count

    def slot(owner):
        return owner % 2 * near_levels + owner // 2 % near_levels

    def window(owner, begin, size):
        at = slot(owner)
        start = at // blocks * slice_rows + begin
        return (
            pl.ds(pl.multiple_of(start, share_rows), size),
            pl.ds(pl.multiple_of(at % blocks * LANES, LANES), LANES),
        )

    def remote(source, target, send, receive, device):
        return pltpu.make_async_remote_copy(
            src_ref=source,
            dst_ref=target,
            send_sem=send,
            recv_sem=receive,
            device_id={"vel": device},
            device_id_type=pl.DeviceIdType.MESH,
        )

    def rail(other):
        return other * 2 + core

    def each_rail(body):
        @pl.loop(1, chips)
        def _(step):
            body(lax.rem(chip + step, chips))

    def each_near(body):
        @pl.loop(1, half)
        def _(step):
            body(near0 + lax.rem(chip - near0 + step, half))

    def greet(device):
        pl.semaphore_signal(
            barrier, inc=1, device_id={"vel": device}, device_id_type=pl.DeviceIdType.MESH
        )

    early = count // 2
    loads = [
        pltpu.make_async_copy(maps.at[pl.ds(0, early)], images.at[pl.ds(0, early)], load_sems.at[0]),
        pltpu.make_async_copy(
            maps.at[pl.ds(early, count - early)], images.at[pl.ds(early, count - early)], load_sems.at[1]
        ),
        pltpu.make_async_copy(vel_in, vel_ref, load_sems.at[2]),
        pltpu.make_async_copy(se_in, se_ref, load_sems.at[3]),
        pltpu.make_async_copy(et_in, et_ref, load_sems.at[4]),
    ]
    barrier = pltpu.get_barrier_semaphore()
    greet(sibling)
    each_rail(lambda other: greet(rail(other)))
    each_near(lambda other: greet(other * 2 + 1 - core))
    greet((far0 + place) * 2 + 1 - core)
    for load in loads:
        load.start()

    span = rows + 2 * EDGE
    relative = (
        lax.broadcasted_iota(jnp.int32, (span, rows), 1)
        - lax.broadcasted_iota(jnp.int32, (span, rows), 0)
        + (EDGE + 1)
    )
    for f in range(4):
        row_taps[f * span : (f + 1) * span, :] = tap_select(relative, SPLINE[f]).astype(jnp.bfloat16)
    base_shape = base.shape[2:]
    for h in range(2):
        distance = (
            lax.broadcasted_iota(jnp.int32, base_shape, 0)
            - lax.broadcasted_iota(jnp.int32, base_shape, 1)
            + (HALO + 1 - REACH - h * LANES)
        )
        for f in range(4):
            base[f, h] = tap_select(distance, SPLINE[f])
    blank = jnp.zeros((blocks, REACH - EDGE, LANES), jnp.float32)

    def filter_rows(source, s, index):
        mixed = jnp.dot(row_taps[...], source[s], preferred_element_type=jnp.float32)
        mixed = mixed.astype(jnp.bfloat16).astype(jnp.float32)
        for f in range(4):
            table[index * 4 + f, :, 0 : REACH - EDGE] = blank
            table[index * 4 + f, :, REACH + rows + EDGE : rows + 2 * REACH] = blank
            for b in range(blocks):
                table[index * 4 + f, b, REACH - EDGE : REACH + rows + EDGE] = mixed[
                    f * span : (f + 1) * span, b * LANES : (b + 1) * LANES
                ]

    loads[0].wait()
    loads[1].wait()
    ready = count * 3 // 4

    @pl.loop(0, ready, step=2)
    def _(s):
        filter_rows(images, s, s)
        filter_rows(images, s + 1, s + 1)

    best_mine[...] = jnp.full_like(best_mine, -jnp.inf)
    for load in loads[2:]:
        load.wait()
    pl.semaphore_wait(barrier, chips + half)

    def vel_copy(source, target, other):
        return remote(vel_ref, vel_all.at[target], vel_send.at[source], vel_recv.at[target], rail(other))

    def swap(s):
        return remote(images.at[s], peer_images.at[s], swap_ssem.at[s], swap_rsem.at[s], sibling)

    @pl.loop(0, count)
    def _(s):
        swap(s).start()

    each_rail(lambda other: vel_copy(other, chip, other).start())
    vel_all[chip, 0, 0] = vel_ref[0, 0]
    vel_all[chip, 0, 1] = vel_ref[0, 1]

    @pl.loop(ready, count, step=2)
    def _(s):
        filter_rows(images, s, s)
        filter_rows(images, s + 1, s + 1)

    @pl.loop(0, count, step=4)
    def _(s):
        for j in range(4):
            swap(s + j).wait_recv()
        for j in range(4):
            filter_rows(peer_images, s + j, s + j + count)

    first = lax.rem(me * count, epochs)
    peer_first = lax.rem(sibling * count, epochs)

    def time(s):
        at = first + s if s < count else peer_first + (s - count)
        return et_ref[se_ref[at]]

    def stack(rate_row, rate_col):
        shifted, weights = [], []
        for s in range(images_all):
            qr = (rate_row * time(s)) >> 5
            qc = (rate_col * time(s)) >> 5
            shifted.append([
                table[s * 4 + (qr & 3), b, pl.ds((qr >> 2) + REACH, rows), :].astype(jnp.bfloat16)
                for b in range(blocks)
            ])
            weights.append(
                jnp.concatenate(
                    [
                        base[qc & 3, h, pl.ds(REACH - (qc >> 2), LANES), :].astype(jnp.bfloat16)
                        for h in range(2)
                    ],
                    axis=1,
                )
            )
        lhs_all = jnp.concatenate(
            [
                jnp.concatenate([shifted[s][b] for s in range(images_all)], axis=1)
                for b in range(blocks)
            ],
            axis=0,
        )
        wide = jnp.dot(lhs_all, jnp.concatenate(weights, axis=0), preferred_element_type=jnp.float32)
        tiles = []
        for t in range(blocks + 1):
            tile = None
            if t < blocks:
                tile = wide[t * rows : (t + 1) * rows, :LANES]
            if t:
                right = wide[(t - 1) * rows : t * rows, LANES:]
                tile = right if tile is None else tile + right
            tiles.append(pltpu.roll(tile, HALO, 1))
        left = lax.broadcasted_iota(jnp.int32, (rows, LANES), 1) < HALO
        return [jnp.where(left, tiles[b], tiles[b + 1]) for b in range(blocks)]

    def part_copy(v, source, other):
        return remote(
            part_send.at[v, slot(other)],
            part_recv.at[v, source - near0],
            part_ssem.at[v, other - near0],
            part_rsem.at[v, source - near0],
            rail(other),
        )

    def far_copy(f):
        return remote(
            far_send.at[f], far_recv.at[f], far_ssem.at[f], far_rsem.at[f], rail(far0 + place)
        )

    def like_copy(o, owner):
        where = window(owner, 0, slice_rows)
        return remote(
            like_send.at[o],
            like_out.at[0, where[0], where[1]],
            like_ssem.at[o],
            like_rsem.at[owner],
            rail(near0 + o),
        )

    def near_sum(v):
        each_near(lambda other: part_copy(v, other, other).wait_recv())
        total = own[v, slot(chip)]
        for step in range(1, half):
            total = total + part_recv[v, lax.rem(place + step, half)].astype(jnp.float32)
        return total

    def forward(f):
        far_send[f] = near_sum(far0 + f).astype(jnp.bfloat16)
        far_copy(f).start()

    def finish_like(o):
        near = near_sum(near0 + o)
        far_copy(o).wait_recv()
        far = far_recv[o].astype(jnp.float32)
        first_kind = near0 == 0
        signal = jnp.where(first_kind, near, far) / spline_norm
        weight = jnp.where(first_kind, far, near) / spline_norm
        value = signal / jnp.sqrt(weight + 1.0)
        best_mine[...] = jnp.maximum(best_mine[...], value)
        like_send[o] = value

    @pl.loop(0, chips)
    def _(i):
        begun = (i + chips - 1) // chips
        later = (i - 1 - half + chips) // chips
        turn = (i - 1 - half) * later
        near_v = near0 + (turn + (turn - place + half) // half) * later + place * (1 - begun)
        is_far = begun - later
        v = is_far * (far0 + i - 1) + (1 - is_far) * near_v

        @pl.when(i >= 1)
        def _():
            vel_copy(v, v, v).wait_recv()

        total = stack(vel_all[v, 0, 0], vel_all[v, 0, 1])
        for at in range(half):
            start = at // blocks * slice_rows
            piece = total[at % blocks][start : start + slice_rows]
            own[v, at] = piece
            part_send[v, at] = piece.astype(jnp.bfloat16)

        each_near(lambda other: part_copy(v, chip, other).start())

        @pl.when(i >= 1 + FORWARD_LAG)
        def _():
            forward(i - 1 - FORWARD_LAG)

    @pl.loop(chips - 1 - FORWARD_LAG, half)
    def _(f):
        forward(f)

    @pl.loop(0, half)
    def _(o):
        finish_like(o)

    other_core = 1 - core
    mine = pl.ds(pl.multiple_of(core * share_rows, share_rows), share_rows)
    theirs = pl.ds(pl.multiple_of(other_core * share_rows, share_rows), share_rows)
    mirror = far0 + place
    meets = [
        remote(best_mine.at[theirs], meet_recv.at[0], meet_ssem.at[0], meet_rsem.at[0], sibling),
        remote(best_mine.at[mine], meet_recv.at[1], meet_ssem.at[1], meet_rsem.at[1], rail(mirror)),
        remote(
            best_mine.at[theirs], meet_recv.at[2], meet_ssem.at[2], meet_rsem.at[2], mirror * 2 + other_core
        ),
    ]
    for meet in (meets[1], meets[2], meets[0]):
        meet.start()
    each_near(lambda other: like_copy(other - near0, chip).start())
    where = window(chip, 0, slice_rows)
    keeps = [
        pltpu.make_async_copy(
            like_send.at[place], like_out.at[0, where[0], where[1]], own_sems.at[0]
        )
    ]
    keeps[0].start()
    for meet in meets:
        meet.wait_recv()
    best = jnp.maximum(best_mine[mine, :], meet_recv[0])
    best_send[...] = jnp.maximum(best, jnp.maximum(meet_recv[1], meet_recv[2]))

    def best_copy(source, target):
        where = window(source // 2, source % 2 * share_rows, share_rows)
        return remote(
            best_send,
            best_out.at[where[0], where[1]],
            best_ssem.at[target],
            best_rsem.at[source],
            near0 * 2 + target,
        )

    seat = place * 2 + core

    def each_seat(body):
        @pl.loop(1, 2 * half)
        def _(step):
            body(lax.rem(seat + step, 2 * half))

    each_seat(lambda target: best_copy(seat, target).start())
    where = window(chip, core * share_rows, share_rows)
    keeps.append(
        pltpu.make_async_copy(best_send, best_out.at[where[0], where[1]], own_sems.at[1])
    )
    keeps[1].start()

    @pl.loop(0, chips)
    def _(v):
        each_near(lambda other: part_copy(v, chip, other).wait_send())

    @pl.loop(0, half)
    def _(f):
        far_copy(f).wait_send()

    @pl.loop(0, count)
    def _(s):
        swap(s).wait_send()

    for keep in keeps:
        keep.wait()
    for meet in meets:
        meet.wait_send()

    each_rail(lambda other: vel_copy(other, chip, other).wait_send())
    each_near(lambda other: like_copy(other - near0, other).wait())
    each_seat(lambda other: best_copy(other, other).wait())


def fused(n, epoch_maps, velocity, slot_epoch, epoch_time):
    count, rows, cols = epoch_maps.shape
    epochs = slot_epoch.shape[0]
    chips = n // 2
    half = chips // 2
    blocks = cols // LANES
    slice_rows = rows * blocks // half
    whole = pl.BlockSpec(memory_space=pl.ANY)
    f32, bf16 = jnp.float32, jnp.bfloat16
    dma = pltpu.SemaphoreType.DMA
    both = pl.pallas_call(
        functools.partial(fused_kernel, chips, epochs, count, rows, cols),
        out_shape=jax.ShapeDtypeStruct((2, rows, cols), f32),
        in_specs=[whole] * 4,
        out_specs=whole,
        scratch_shapes=[
            pltpu.SMEM((epochs,), jnp.int32),
            pltpu.SMEM((epochs,), jnp.int32),
            pltpu.SMEM((1, 2), jnp.int32),
            pltpu.VMEM((count, rows, cols), bf16),
            pltpu.VMEM((count, rows, cols), bf16),
            pltpu.VMEM((4 * (rows + 2 * EDGE), rows), bf16),
            pltpu.VMEM((2 * count * 4, blocks, rows + 2 * REACH, LANES), f32),
            pltpu.VMEM((4, 2, LANES + 2 * REACH, LANES), f32),
            pltpu.SMEM((chips, 1, 2), jnp.int32),
            pltpu.VMEM((chips, half, slice_rows, LANES), bf16),
            pltpu.VMEM((chips, half, slice_rows, LANES), bf16),
            pltpu.VMEM((chips, half, slice_rows, LANES), f32),
            pltpu.VMEM((half, slice_rows, LANES), bf16),
            pltpu.VMEM((half, slice_rows, LANES), bf16),
            pltpu.VMEM((half, slice_rows, LANES), f32),
            pltpu.VMEM((slice_rows, LANES), f32),
            pltpu.VMEM((3, slice_rows // 2, LANES), f32),
            pltpu.VMEM((slice_rows // 2, LANES), f32),
            dma((5,)),
            dma((2,)),
            dma((count,)),
            dma((count,)),
            dma((chips,)),
            dma((chips,)),
            dma((chips, half)),
            dma((chips, half)),
            dma((half,)),
            dma((half,)),
            dma((3,)),
            dma((3,)),
            dma((half,)),
            dma((chips,)),
            dma((2 * half,)),
            dma((2 * half,)),
        ],
        compiler_params=pltpu.CompilerParams(collective_id=0, has_side_effects=True),
    )(slot_epoch, epoch_time, velocity, epoch_maps)
    return (both[:1], both[1])


def fits(n, epoch_maps, velocity, epochs):
    count, rows, cols = epoch_maps.shape
    chips = n // 2
    blocks = cols // LANES
    return (
        n % 8 == 0
        and count % 4 == 0
        and velocity.shape[0] == 1
        and n * count == 2 * epochs
        and cols % LANES == 0
        and chips // 2 % blocks == 0
        and rows % (chips // 2 // blocks * 16) == 0
        and rows * cols * count <= FIT_PIXELS
    )


def local(n, epoch_maps, velocity, slot_epoch, epoch_time):
    count, rows, cols = epoch_maps.shape
    epochs = slot_epoch.shape[0]
    if fits(n, epoch_maps, velocity, epochs):
        return fused(n, epoch_maps, velocity, slot_epoch, epoch_time)
    me = lax.axis_index("vel")
    vels = lax.all_gather(velocity, "vel", axis=0, tiled=True)
    first = lax.rem(me * count, epochs)
    slots = lax.dynamic_slice_in_dim(slot_epoch, first, count, 0)
    times = epoch_time[slots]
    partial = pl.pallas_call(
        functools.partial(stack_kernel, count, rows, cols),
        out_shape=jax.ShapeDtypeStruct((vels.shape[0], rows, cols), jnp.bfloat16),
        in_specs=[
            pl.BlockSpec(memory_space=pltpu.SMEM),
            pl.BlockSpec(memory_space=pltpu.SMEM),
            pl.BlockSpec(memory_space=pltpu.VMEM),
        ],
        out_specs=pl.BlockSpec(memory_space=pltpu.VMEM),
        scratch_shapes=[
            pltpu.VMEM((count, rows, cols + 2 * HALO), jnp.bfloat16),
            pltpu.VMEM((count * 2 * LANES, LANES), jnp.bfloat16),
            pltpu.VMEM((count, rows, cols + 2 * HALO), jnp.bfloat16),
        ],
    )(vels, times, epoch_maps)
    mine = velocity.shape[0]
    received = lax.all_to_all(partial, "vel", 0, 0, tiled=True)
    received = received.reshape(2, n // 2, mine, rows, cols)
    stack_sums = jnp.sum(received.astype(jnp.float32), axis=1) / spline_norm
    likelihood = stack_sums[0] / jnp.sqrt(stack_sums[1] + 1.0)
    best_value = lax.pmax(jnp.max(likelihood, axis=0), "vel")
    return (likelihood, best_value)


def solution(mesh):
    return jax.shard_map(
        functools.partial(local, mesh.shape["vel"]),
        mesh=mesh,
        in_specs=(P("vel", "groups", None), P("vel", None), P(), P()),
        out_specs=(P("vel", "groups", None), P("groups", None)),
        check_vma=False,
    )
```
